256 devices in a mesh: section: 2 (over core), tp: 8 (over z), mem: 16 (over y, x).
Axes of the slice: x: 4, y: 4, z: 8, core: 2. Of those that a mesh axis runs over, the one named last changes fastest.
Arguments:
- hidden_in: bfloat16 [32, 8192], P(None, 'mem'), may hold values from -12 to 12
- lengths: int32 [32], replicated, may hold values from 1 to 4096, as said below
- owner_order: int32 [32], replicated, may hold values from 0 to 31, each once
- attn_gain: bfloat16 [2, 8192], P('section', 'mem'), may hold values from 0.25 to 1.75
- w_query: bfloat16 [2, 8192, 8192], P('section', 'mem', 'tp'), may hold values from -0.0625 to 0.0625
- w_key: bfloat16 [2, 8192, 1024], P('section', 'mem', 'tp'), may hold values from -0.0625 to 0.0625
- w_value: bfloat16 [2, 8192, 1024], P('section', 'mem', 'tp'), may hold values from -0.0625 to 0.0625
- w_out: bfloat16 [2, 8192, 8192], P('section', 'tp', 'mem'), may hold values from -0.0625 to 0.0625
- ffn_gain: bfloat16 [2, 8192], P('section', 'mem'), may hold values from 0.25 to 1.75
- w_gate: bfloat16 [2, 8192, 14336], P('section', 'mem', 'tp'), may hold values from -0.0625 to 0.0625
- w_up: bfloat16 [2, 8192, 14336], P('section', 'mem', 'tp'), may hold values from -0.0625 to 0.0625
- w_down: bfloat16 [2, 14336, 8192], P('section', 'tp', 'mem'), may hold values from -0.046875 to 0.046875
- key_cache: bfloat16 [2, 32, 4096, 1024], P('section', 'mem', None, 'tp'), may hold values from -250 to 250
- value_cache: bfloat16 [2, 32, 4096, 1024], P('section', 'mem', None, 'tp'), may hold values from -12 to 12
Outputs:
- layer_outputs: bfloat16 [2, 32, 8192], P('section', None, 'mem')
The draws below stay inside these ranges and needn't reach their ends.
Inputs may be any that keep to these rules, and one draw needn't show every extreme that they name: Request r has lengths[r] filled positions in its cache; the largest length is exactly 4096. Cache slot j holds request owner_order[j]; index m of mem holds slots m * 2 to (m + 1) * 2 - 1.
All inputs are finite; a program needn't handle non-finite values.
Results may differ from the reference program's by a relative error of at most 0.014.
Values may be sent and summed in bfloat16 or wider, within the bound.
A program may use at most 64 MiB of HBM per device.

```python
import math
import jax
import jax.numpy as jnp
from jax import lax

D = 8192
HQ = 64
KVH = 8
HD = 128
FF = 14336
CTX = 4096
BATCH = 32
LAYERS = 2


def draw_hidden_in(key, part):
    first = jax.random.fold_in(key, 0)
    base = jax.random.normal(first, (BATCH, D), jnp.float32)
    ramp = 0.5 * 3.0 ** (jnp.arange(D, dtype=jnp.float32) / D)
    values = base * ramp[None, :]
    return jnp.clip(values, -12.0, 12.0).astype(jnp.bfloat16)


def draw_lengths(key, part):
    first, second, third = jax.random.split(key, 3)
    levels = max(int(math.log2(CTX)), 1)
    powers = jax.random.randint(first, (BATCH,), 0, levels)
    lowest = jnp.left_shift(jnp.ones((BATCH,), jnp.int32), powers)
    extra = jax.random.randint(second, (BATCH,), 0, CTX)
    drawn = lowest + extra % lowest
    longest = jax.random.randint(third, (), 0, BATCH)
    return jnp.where(jnp.arange(BATCH) == longest, CTX, jnp.minimum(drawn, CTX)).astype(jnp.int32)


def draw_key_cache(key, part):
    first = jax.random.fold_in(key, 0)
    shape = (LAYERS, BATCH, CTX, KVH * HD)
    base = jnp.clip(jax.random.normal(first, shape, jnp.float32), -6.0, 6.0)
    values = base
    return values.astype(jnp.bfloat16)


def draw_value_cache(key, part):
    first, second = jax.random.split(key, 2)
    shape = (LAYERS, BATCH, CTX, KVH * HD)
    level = jax.random.normal(first, (LAYERS, BATCH, 1, KVH * HD), jnp.float32)
    values = level + 2.0 * jnp.clip(jax.random.normal(second, shape, jnp.float32), -4.5, 4.5)
    return jnp.clip(values, -12.0, 12.0).astype(jnp.bfloat16)


def shard_levels(stream_key, shape, pieces, low, high):
    def one(dim, blocks):
        heights = jax.random.uniform(jax.random.fold_in(jax.random.fold_in(stream_key, 6), dim), (blocks,), jnp.float32, low / len(pieces), high / len(pieces))
        return jnp.repeat(jnp.exp(heights), shape[dim] // blocks).reshape((-1,) + (1,) * (len(shape) - dim - 1))

    factor_of = one(*pieces[0])
    for cut in pieces[1:]:
        factor_of = factor_of * one(*cut)
    return factor_of


def scatter_about(stream_key, extent, width, reach, pieces=(), held_as=jnp.bfloat16):
    factor_of = shard_levels(stream_key, extent, pieces, -0.22, 0.18) if pieces else 1.0
    values = jax.random.normal(stream_key, extent, jnp.float32) * width * factor_of
    return jnp.minimum(jnp.maximum(values, -reach), reach).astype(held_as)


def setup_inputs(seed: int = 0) -> dict:
    arg_keys = jax.random.split(jax.random.key(seed), 15)
    hidden_in = draw_hidden_in(jax.random.fold_in(arg_keys[14], 71), 0)
    lengths = draw_lengths(jax.random.fold_in(arg_keys[14], 71), 0)
    owner_order = jax.random.permutation(arg_keys[2], BATCH).astype(jnp.int32)
    attn_gain = jnp.clip(1.0 + 0.15 * jax.random.normal(arg_keys[3], (LAYERS, D), jnp.float32), 0.25, 1.75).astype(jnp.bfloat16)
    w_query = scatter_about(arg_keys[4], (LAYERS, D, HQ * HD), D ** -0.5, 0.0625, ((0, 2), (1, 16), (2, 8)))
    w_key = scatter_about(arg_keys[5], (LAYERS, D, KVH * HD), D ** -0.5, 0.0625, ((0, 2), (1, 16), (2, 8)))
    w_value = scatter_about(arg_keys[6], (LAYERS, D, KVH * HD), D ** -0.5, 0.0625, ((0, 2), (1, 16), (2, 8)))
    w_out = scatter_about(arg_keys[7], (LAYERS, HQ * HD, D), (HQ * HD) ** -0.5, 0.0625, ((0, 2), (1, 8), (2, 16)))
    ffn_gain = jnp.clip(1.0 + 0.15 * jax.random.normal(arg_keys[8], (LAYERS, D), jnp.float32), 0.25, 1.75).astype(jnp.bfloat16)
    w_gate = scatter_about(arg_keys[9], (LAYERS, D, FF), D ** -0.5, 0.0625, ((0, 2), (1, 16), (2, 8)))
    w_up = scatter_about(arg_keys[10], (LAYERS, D, FF), D ** -0.5, 0.0625, ((0, 2), (1, 16), (2, 8)))
    w_down = scatter_about(arg_keys[11], (LAYERS, FF, D), FF ** -0.5, 0.046875, ((0, 2), (1, 8), (2, 16)))
    key_cache = draw_key_cache(jax.random.fold_in(arg_keys[14], 71), 0)
    value_cache = draw_value_cache(jax.random.fold_in(arg_keys[14], 71), 0)
    return dict(hidden_in=hidden_in, lengths=lengths, owner_order=owner_order, attn_gain=attn_gain, w_query=w_query, w_key=w_key, w_value=w_value, w_out=w_out, ffn_gain=ffn_gain, w_gate=w_gate, w_up=w_up, w_down=w_down, key_cache=key_cache, value_cache=value_cache)


epsilon = 1e-05
rope_base = 500000.0

def rotate(vectors, positions):
    size = vectors.shape[-1]
    half = size // 2
    freqs = rope_base ** (-(jnp.arange(half, dtype=jnp.float32) * 2.0) / size)
    angles = positions[:, None, None] * freqs[None, None, :]
    cosine = jnp.concatenate([jnp.cos(angles), jnp.cos(angles)], axis=-1)
    sine = jnp.concatenate([jnp.sin(angles), jnp.sin(angles)], axis=-1)
    turned = jnp.concatenate([-vectors[..., half:], vectors[..., :half]], axis=-1)
    return vectors * cosine + turned * sine

def scale_rows(states, norm_gain):
    as_float = states.astype(jnp.float32)
    factor = lax.rsqrt(lax.optimization_barrier(jnp.sum(as_float * as_float, axis=1)) / as_float.shape[1] + epsilon)
    scaled = (as_float * norm_gain.astype(jnp.float32)[None, :]).astype(jnp.bfloat16)
    return (scaled, factor)

def attend_one(request_item):
    queries, new_key, new_value, key_rows, value_rows, length = request_item
    kv_heads = new_key.shape[0]
    context = key_rows.shape[0]
    keys_float = key_rows.reshape(context, kv_heads, HD).astype(jnp.float32)
    values_float = value_rows.reshape(context, kv_heads, HD).astype(jnp.float32)
    queries_float = queries.astype(jnp.float32)
    score_scale = 1.0 / math.sqrt(HD)
    scores = jnp.einsum('grd,jgd->grj', queries_float, keys_float) * score_scale
    live_slots = jnp.arange(context, dtype=jnp.int32) < length
    scores = jnp.where(live_slots[None, None, :], scores, -jnp.inf)
    own_score = jnp.einsum('grd,gd->gr', queries_float, new_key.astype(jnp.float32)) * score_scale
    peak_score = jnp.maximum(lax.optimization_barrier(jnp.max(scores, axis=-1)), own_score)
    soft_weights = jnp.exp(scores - peak_score[..., None])
    own_weight = jnp.exp(own_score - peak_score)
    softmax_total = lax.optimization_barrier(jnp.sum(soft_weights, axis=-1)) + own_weight
    soft_rounded = lax.optimization_barrier(soft_weights.astype(jnp.bfloat16)).astype(jnp.float32)
    own_rounded = lax.optimization_barrier(own_weight.astype(jnp.bfloat16)).astype(jnp.float32)
    mixed_heads = jnp.einsum('grj,jgd->grd', soft_rounded, values_float)
    mixed_heads = mixed_heads + own_rounded[..., None] * new_value.astype(jnp.float32)[:, None, :]
    return (mixed_heads / softmax_total[..., None]).astype(jnp.bfloat16)

def decoder_layer(states, lengths, owner_order, attn_gain, w_query, w_key, w_value, w_out, ffn_gain, w_gate, w_up, w_down, key_rows, value_rows):
    request_count = states.shape[0]
    kv_heads = w_key.shape[1] // HD
    group_size = w_query.shape[1] // w_key.shape[1]
    scaled, factor = scale_rows(states, attn_gain)
    queries = (jnp.dot(scaled, w_query, preferred_element_type=jnp.float32) * factor[:, None]).reshape(request_count, -1, HD)
    new_keys = (jnp.dot(scaled, w_key, preferred_element_type=jnp.float32) * factor[:, None]).reshape(request_count, kv_heads, HD)
    new_values = (jnp.dot(scaled, w_value, preferred_element_type=jnp.float32) * factor[:, None]).reshape(request_count, kv_heads, HD)
    positions = lengths.astype(jnp.float32)
    queries = rotate(queries, positions).astype(jnp.bfloat16)
    new_keys = rotate(new_keys, positions).astype(jnp.bfloat16)
    new_values = new_values.astype(jnp.bfloat16)
    slot_queries = jnp.take(queries, owner_order, axis=0).reshape(request_count, kv_heads, group_size, HD)
    slot_keys = jnp.take(new_keys, owner_order, axis=0)
    slot_values = jnp.take(new_values, owner_order, axis=0)
    slot_lengths = jnp.take(lengths, owner_order, axis=0)
    attended = lax.map(attend_one, (slot_queries, slot_keys, slot_values, key_rows, value_rows, slot_lengths))
    attended = attended.reshape(request_count, -1)
    request_rows = jnp.zeros_like(attended).at[owner_order].set(attended)
    attention_out = jnp.dot(request_rows, w_out, preferred_element_type=jnp.float32)
    after_attention = (states.astype(jnp.float32) + attention_out).astype(jnp.bfloat16)
    scaled_second, factor_second = scale_rows(after_attention, ffn_gain)
    gate_sums = jnp.dot(scaled_second, w_gate, preferred_element_type=jnp.float32) * factor_second[:, None]
    up_sums = jnp.dot(scaled_second, w_up, preferred_element_type=jnp.float32) * factor_second[:, None]
    hidden = (jax.nn.silu(gate_sums) * up_sums).astype(jnp.bfloat16)
    down_terms = jnp.dot(hidden, w_down, preferred_element_type=jnp.float32)
    return (after_attention.astype(jnp.float32) + down_terms).astype(jnp.bfloat16)

def reference(hidden_in, lengths, owner_order, attn_gain, w_query, w_key, w_value, w_out, ffn_gain, w_gate, w_up, w_down, key_cache, value_cache):
    states = hidden_in
    results = []
    for layer_index in range(LAYERS):
        states = decoder_layer(states, lengths, owner_order, attn_gain[layer_index], w_query[layer_index], w_key[layer_index], w_value[layer_index], w_out[layer_index], ffn_gain[layer_index], w_gate[layer_index], w_up[layer_index], w_down[layer_index], key_cache[layer_index], value_cache[layer_index])
        results.append(states)
    return jnp.stack(results)
```

```python
import functools
import math

import jax
import jax.numpy as jnp
import numpy as np
from jax import lax
from jax.experimental import pallas as pl
from jax.experimental.pallas import tpu as pltpu
from jax.sharding import PartitionSpec as P

D = 8192
HD = 128
CTX = 4096
ROWS = 32
EPS = 1e-05
MESH = pl.DeviceIdType.MESH
F32 = jnp.float32
BF16 = jnp.bfloat16


def _hops(o):
    return min(o[0], 4 - o[0]) + min(o[1], 4 - o[1])


OFFSETS = sorted(
    [(a, b) for a in range(4) for b in range(4) if (a, b) != (0, 0)], key=lambda o: -_hops(o)
)
RING = (4, 3, 5, 2, 6, 1, 7)
OWNERS = 14


def _nt(a, b):
    return lax.dot_general(a, b, (((1,), (1,)), ((), ())), preferred_element_type=F32)


def _nn(a, b):
    return jnp.dot(a, b, preferred_element_type=F32)


def kernel(
    lengths,
    owner,
    freqs,
    hidden_in,
    attn_gain,
    ffn_gain,
    w_query,
    w_key,
    w_value,
    w_out,
    w_gate,
    w_up,
    w_down,
    key_cache,
    value_cache,
    out,
    wqkv,
    wo,
    wg,
    wu,
    wd,
    kbuf,
    vbuf,
    xin,
    xout,
    sb1,
    rb1,
    sb2,
    rb2,
    fb2,
    sb3,
    rb3,
    ssq,
    rsq,
    sb4,
    rb4,
    sb5,
    rb5,
    sb6,
    rb6,
    wsem,
    send,
    recv,
):
    sec = lax.axis_index("section")
    tp = lax.axis_index("tp")
    mem = lax.axis_index("mem")
    my, mx = mem // 4, lax.rem(mem, 4)

    def peer(o):
        return lax.rem(my + o[0], 4) * 4 + lax.rem(mx + o[1], 4)

    def slot_at(o):
        return ((4 - o[0]) % 4) * 4 + (4 - o[1]) % 4

    loads = [
        (w_query.at[0], wqkv.at[:, pl.ds(0, 1024)]),
        (w_key.at[0], wqkv.at[:, pl.ds(1024, 128)]),
        (w_value.at[0], wqkv.at[:, pl.ds(1152, 128)]),
        (key_cache.at[0, 0], kbuf.at[:, pl.ds(0, 128)]),
        (key_cache.at[0, 1], kbuf.at[:, pl.ds(128, 128)]),
        (value_cache.at[0, 0], vbuf.at[:, pl.ds(0, 128)]),
        (value_cache.at[0, 1], vbuf.at[:, pl.ds(128, 128)]),
        (w_out.at[0], wo),
        (w_gate.at[0], wg),
        (w_up.at[0], wu),
        (w_down.at[0], wd),
    ]
    loads = [pltpu.make_async_copy(s, d, wsem.at[i]) for i, (s, d) in enumerate(loads)]
    for c in loads[:3]:
        c.start()

    barrier = pltpu.get_barrier_semaphore()
    for o in OFFSETS:
        pl.semaphore_signal(barrier, inc=1, device_id={"mem": peer(o)}, device_id_type=MESH)
    for k in RING:
        pl.semaphore_signal(
            barrier, inc=1, device_id={"tp": lax.rem(tp + k, 8)}, device_id_type=MESH
        )
    pl.semaphore_signal(barrier, inc=1, device_id={"section": 1 - sec}, device_id_type=MESH)
    for c in loads[3:]:
        c.start()

    row = lax.broadcasted_iota(jnp.int32, (ROWS, ROWS), 0)
    col = lax.broadcasted_iota(jnp.int32, (ROWS, ROWS), 1)
    by_row = jnp.zeros((ROWS, ROWS), jnp.int32)
    by_col = jnp.zeros((ROWS, ROWS), jnp.int32)
    for j in range(ROWS):
        r = owner[j]
        by_row = jnp.where(row == j, r, by_row)
        by_col = jnp.where(col == j, r, by_col)
    to_slots = jnp.where(by_row == col, 1.0, 0.0).astype(BF16)
    to_requests = jnp.where(by_col == row, 1.0, 0.0).astype(BF16)

    len0 = lengths[owner[2 * mem]]
    len1 = lengths[owner[2 * mem + 1]]
    upper = lax.broadcasted_iota(jnp.int32, (8, 128), 0) < 4
    angles = jnp.where(upper, len0, len1).astype(F32) * freqs[...]
    cosine = jnp.cos(angles)
    sine = jnp.sin(angles)
    lane = lax.broadcasted_iota(jnp.int32, (8, 128), 1)
    sine = jnp.where(lane < 64, -sine, sine)

    @pl.when(sec == 0)
    def _():
        xin[...] = _nn(to_slots, hidden_in[...]).astype(BF16)

    pl.semaphore_wait(barrier, 23)

    @pl.when(sec == 1)
    def _():
        pltpu.make_async_copy(xout, xin, recv.at[7]).wait()

    x = xin[...].astype(F32)
    scaled = (x * attn_gain[...].astype(F32)).astype(BF16)
    squares = jnp.sum(x * x, axis=1, keepdims=True)
    for c in loads[:3]:
        c.wait()
    part = _nn(scaled, wqkv[...])
    for h in range(10):
        sb1[pl.ds(h, ROWS, stride=12), :] = part[:, h * 128 : (h + 1) * 128]
    sb1[pl.ds(10, ROWS, stride=12), :] = jnp.broadcast_to(squares, (ROWS, 128))
    sb1[pl.ds(11, ROWS, stride=12), :] = jnp.zeros((ROWS, 128), F32)

    def rows_of(m):
        return pl.ds(pl.multiple_of(m * 24, 8), 24)

    for o in OFFSETS:
        pltpu.make_async_remote_copy(
            src_ref=sb1.at[rows_of(peer(o))],
            dst_ref=rb1.at[slot_at(o)],
            send_sem=send.at[0],
            recv_sem=recv.at[0],
            device_id={"mem": peer(o)},
            device_id_type=MESH,
        ).start()
    heads = sb1[rows_of(mem), :]
    from15 = pl.ds(1, 15)
    pltpu.make_async_copy(rb1.at[from15], rb1.at[from15], recv.at[0]).wait()
    for k in range(1, 16):
        heads = heads + rb1[k]

    def turned(v, s):
        c, n = cosine[4 * s : 4 * s + 1], sine[4 * s : 4 * s + 1]
        return v * c + pltpu.roll(v, 64, 1) * n

    scale = 1.0 / math.sqrt(HD)
    zero = jnp.zeros((8, 128), F32)
    queries, owns, values = [], [], []
    for s in range(2):
        mine = heads[12 * s : 12 * s + 12]
        mine = mine * lax.rsqrt(mine[10:11] / D + EPS)
        q = turned(mine[0:8], s)
        kv = turned(mine[8:9], s).astype(BF16).astype(F32)
        values.append(jnp.broadcast_to(mine[9:10].astype(BF16).astype(F32), (8, 128)))
        q = q.astype(BF16).astype(F32)
        owns.append(jnp.sum(q * kv, axis=1, keepdims=True) * scale)
        queries.append(jnp.concatenate([q, zero] if s == 0 else [zero, q], axis=1))
    queries = jnp.concatenate(queries, axis=0).astype(BF16)
    own_score = jnp.concatenate(owns, axis=0)
    new_values = jnp.concatenate(values, axis=0)
    loads[3].wait()
    loads[4].wait()
    scores = _nt(queries, kbuf[...]) * scale
    where = lax.broadcasted_iota(jnp.int32, (16, CTX), 1)
    first = lax.broadcasted_iota(jnp.int32, (16, 1), 0) < 8
    scores = jnp.where(where < jnp.where(first, len0, len1), scores, -jnp.inf)
    peak = jnp.maximum(jnp.max(scores, axis=1, keepdims=True), own_score)
    soft = jnp.exp(scores - peak)
    own = jnp.exp(own_score - peak)
    total = jnp.sum(soft, axis=1, keepdims=True) + own
    loads[5].wait()
    loads[6].wait()
    mixed = _nn(soft.astype(BF16), vbuf[...])
    mixed = jnp.where(first, mixed[:, :128], mixed[:, 128:])
    mixed = mixed + own.astype(BF16).astype(F32) * new_values
    attended = (mixed / total).astype(BF16)
    sb2[...] = attended
    rb2[mem] = attended
    for o in OFFSETS:
        pltpu.make_async_remote_copy(
            src_ref=sb2,
            dst_ref=rb2.at[mem],
            send_sem=send.at[1],
            recv_sem=recv.at[1],
            device_id={"mem": peer(o)},
            device_id_type=MESH,
        ).start()
    loads[7].wait()
    pltpu.make_async_copy(rb2.at[from15], rb2.at[from15], recv.at[1]).wait()
    fb2[...] = rb2[...].astype(F32).reshape(256, 128)
    wide = jnp.concatenate([fb2[pl.ds(h, ROWS, stride=8), :] for h in range(8)], axis=1)
    part = _nn(wide.astype(BF16), wo[...])

    from7 = pl.ds(1, 7)

    def tp_sum(part, sb, rb, which):
        sb[...] = part.astype(BF16)
        for k in RING:
            pltpu.make_async_remote_copy(
                src_ref=sb,
                dst_ref=rb.at[tp],
                send_sem=send.at[which],
                recv_sem=recv.at[which],
                device_id={"tp": lax.rem(tp + k, 8)},
                device_id_type=MESH,
            ).start()
        rb[tp] = sb[...]
        pltpu.make_async_copy(rb.at[from7], rb.at[from7], recv.at[which]).wait()
        total = rb[0].astype(F32)
        for k in range(1, 8):
            total = total + rb[k].astype(F32)
        return total

    x = (x + tp_sum(part, sb3, rb3, 2)).astype(BF16).astype(F32)

    squares = jnp.sum(x * x, axis=1, keepdims=True)
    packed = jnp.zeros((8, 128), F32)
    for g in range(4):
        packed = jnp.where(lane // 32 == g, squares[8 * g : 8 * g + 8], packed)
    ssq[...] = packed
    for o in OFFSETS:
        pltpu.make_async_remote_copy(
            src_ref=ssq,
            dst_ref=rsq.at[slot_at(o)],
            send_sem=send.at[3],
            recv_sem=recv.at[3],
            device_id={"mem": peer(o)},
            device_id_type=MESH,
        ).start()
    scaled = (x * ffn_gain[...].astype(F32)).astype(BF16)
    loads[8].wait()
    loads[9].wait()

    def columns(j):
        return pl.ds(pl.multiple_of(j * 128, 128), 128)

    def units(j):
        j = jnp.minimum(j, OWNERS - 1)
        both = jnp.concatenate([wg[:, columns(j)], wu[:, columns(j)]], axis=1)
        return _nn(scaled, both)

    groups = (OFFSETS[:5], OFFSETS[5:11], OFFSETS[11:])
    for group in groups:
        for o in group:
            sb4[o[0] * 4 + o[1]] = units(peer(o)).astype(BF16)
        for o in group:

            @pl.when(peer(o) < OWNERS)
            def _(o=o):
                pltpu.make_async_remote_copy(
                    src_ref=sb4.at[o[0] * 4 + o[1]],
                    dst_ref=rb4.at[slot_at(o)],
                    send_sem=send.at[4],
                    recv_sem=recv.at[4],
                    device_id={"mem": peer(o)},
                    device_id_type=MESH,
                ).start()

    sums = units(mem)
    pltpu.make_async_copy(rsq.at[from15], rsq.at[from15], recv.at[3]).wait()
    for k in range(1, 16):
        packed = packed + rsq[k]
    packed = lax.rsqrt(packed / D + EPS)
    factor = jnp.concatenate([packed[:, 32 * g : 32 * g + 1] for g in range(4)], axis=0)

    @pl.when(mem < OWNERS)
    def _():
        pltpu.make_async_copy(rb4.at[from15], rb4.at[from15], recv.at[4]).wait()
        own_units = sums
        for k in range(1, 16):
            own_units = own_units + rb4[k].astype(F32)
        own_units = own_units * factor
        gate, up = own_units[:, :128], own_units[:, 128:]
        units_here = (gate / (1.0 + jnp.exp(-gate)) * up).astype(BF16)
        sb5[...] = units_here
        rb5[mem] = units_here
        for o in OFFSETS:
            pltpu.make_async_remote_copy(
                src_ref=sb5,
                dst_ref=rb5.at[mem],
                send_sem=send.at[5],
                recv_sem=recv.at[5],
                device_id={"mem": peer(o)},
                device_id_type=MESH,
            ).start()
        from13 = pl.ds(0, 13)
        pltpu.make_async_copy(rb5.at[from13], rb5.at[from13], recv.at[5]).wait()

    @pl.when(mem >= OWNERS)
    def _():
        from14 = pl.ds(0, 14)
        pltpu.make_async_copy(rb5.at[from14], rb5.at[from14], recv.at[5]).wait()

    loads[10].wait()
    hidden = jnp.concatenate([rb5[j] for j in range(OWNERS)], axis=1)
    part = _nn(hidden, wd[...])
    x = (x + tp_sum(part, sb6, rb6, 6)).astype(BF16)
    xout[...] = x

    across = pltpu.make_async_remote_copy(
        src_ref=xout,
        dst_ref=xin,
        send_sem=send.at[7],
        recv_sem=recv.at[7],
        device_id={"section": 1 - sec},
        device_id_type=MESH,
    )

    @pl.when(sec == 0)
    def _():
        across.start()

    out[0] = _nn(to_requests, x).astype(BF16)

    pltpu.make_async_copy(rb1.at[from15], rb1.at[from15], send.at[0]).wait()
    pltpu.make_async_copy(rb2.at[from15], rb2.at[from15], send.at[1]).wait()
    pltpu.make_async_copy(rb3.at[from7], rb3.at[from7], send.at[2]).wait()
    pltpu.make_async_copy(rsq.at[from15], rsq.at[from15], send.at[3]).wait()
    pltpu.make_async_copy(rb6.at[from7], rb6.at[from7], send.at[6]).wait()

    @pl.when(mem < OWNERS)
    def _():
        from13 = pl.ds(0, 13)
        pltpu.make_async_copy(rb4.at[from13], rb4.at[from13], send.at[4]).wait()
        all15 = pl.ds(0, 15)
        pltpu.make_async_copy(rb5.at[all15], rb5.at[all15], send.at[5]).wait()

    @pl.when(mem >= OWNERS)
    def _():
        from14 = pl.ds(0, 14)
        pltpu.make_async_copy(rb4.at[from14], rb4.at[from14], send.at[4]).wait()

    @pl.when(sec == 0)
    def _():
        across.wait_send()


FREQS = (500000.0 ** (-(np.arange(64, dtype=np.float64) * 2.0) / 128)).astype(np.float32)
FREQS = np.concatenate([FREQS, FREQS])[None, :]


def per_device(hidden_in, lengths, owner_order, attn_gain, w_query, w_key, w_value, w_out,
               ffn_gain, w_gate, w_up, w_down, key_cache, value_cache):
    smem = pl.BlockSpec(memory_space=pltpu.SMEM)
    vmem = pl.BlockSpec(memory_space=pltpu.VMEM)
    hbm = pl.BlockSpec(memory_space=pl.ANY)
    V = pltpu.VMEM
    return pl.pallas_call(
        kernel,
        out_shape=jax.ShapeDtypeStruct((1, ROWS, 512), BF16),
        in_specs=[smem, smem, vmem, vmem, vmem, vmem] + [hbm] * 9,
        out_specs=vmem,
        scratch_shapes=[
            V((512, 1280), BF16),
            V((1024, 512), BF16),
            V((512, 1792), BF16),
            V((512, 1792), BF16),
            V((1792, 512), BF16),
            V((CTX, 256), BF16),
            V((CTX, 256), BF16),
            V((ROWS, 512), BF16),
            V((ROWS, 512), BF16),
            V((384, 128), F32),
            V((16, 24, 128), F32),
            V((16, 128), BF16),
            V((16, 16, 128), BF16),
            V((256, 128), F32),
            V((ROWS, 512), BF16),
            V((8, ROWS, 512), BF16),
            V((8, 128), F32),
            V((16, 8, 128), F32),
            V((16, ROWS, 256), BF16),
            V((16, ROWS, 256), BF16),
            V((ROWS, 128), BF16),
            V((16, ROWS, 128), BF16),
            V((ROWS, 512), BF16),
            V((8, ROWS, 512), BF16),
            pltpu.SemaphoreType.DMA((11,)),
            pltpu.SemaphoreType.DMA((8,)),
            pltpu.SemaphoreType.DMA((8,)),
        ],
        compiler_params=pltpu.CompilerParams(
            collective_id=0, has_side_effects=True, vmem_limit_bytes=56 << 20
        ),
    )(
        lengths, owner_order, jnp.asarray(FREQS), hidden_in, attn_gain, ffn_gain,
        w_query, w_key, w_value, w_out, w_gate, w_up, w_down, key_cache, value_cache,
    )


def solution(mesh):
    placed = (
        P(None, "mem"),
        P(),
        P(),
        P("section", "mem"),
        P("section", "mem", "tp"),
        P("section", "mem", "tp"),
        P("section", "mem", "tp"),
        P("section", "tp", "mem"),
        P("section", "mem"),
        P("section", "mem", "tp"),
        P("section", "mem", "tp"),
        P("section", "tp", "mem"),
        P("section", "mem", None, "tp"),
        P("section", "mem", None, "tp"),
    )
    return jax.shard_map(
        per_device, mesh=mesh, in_specs=placed, out_specs=P("section", None, "mem"), check_vma=False
    )
```

```python
import functools
import math

import jax
import jax.numpy as jnp
import numpy as np
from jax import lax
from jax.experimental import pallas as pl
from jax.experimental.pallas import tpu as pltpu
from jax.sharding import PartitionSpec as P

D = 8192
HD = 128
CTX = 4096
ROWS = 32
EPS = 1e-05
MESH = pl.DeviceIdType.MESH
F32 = jnp.float32
BF16 = jnp.bfloat16


def _hops(o):
    return min(o[0], 4 - o[0]) + min(o[1], 4 - o[1])


OFFSETS = sorted(
    [(a, b) for a in range(4) for b in range(4) if (a, b) != (0, 0)], key=lambda o: -_hops(o)
)
RING = (4, 3, 5, 2, 6, 1, 7)
BARRIER = 15 + 7 + 8
OWNERS = 14


def _nt(a, b):
    return lax.dot_general(a, b, (((1,), (1,)), ((), ())), preferred_element_type=F32)


def _nn(a, b):
    return jnp.dot(a, b, preferred_element_type=F32)


def kernel(
    lengths_in,
    owner_in,
    freqs_in,
    hidden_in,
    attn_gain_in,
    ffn_gain_in,
    w_query,
    w_key,
    w_value,
    w_out,
    w_gate,
    w_up,
    w_down,
    key_cache,
    value_cache,
    out,
    lengths,
    owner,
    freqs,
    hidden,
    attn_gain,
    ffn_gain,
    wqkv,
    wo,
    wg,
    wu,
    wd,
    kbuf,
    vbuf,
    xin,
    xout,
    x2,
    x2in,
    sb1,
    rb1,
    sb2,
    rb2,
    fb2,
    sb3,
    rb3,
    ssq,
    rsq,
    sb4,
    rb4,
    sb5,
    rb5,
    sb6,
    rb6,
    ssem,
    wsem,
    send,
    recv,
    recv4,
    recv5,
    recv6,
):
    sec = lax.axis_index("section")
    tp = lax.axis_index("tp")
    mem = lax.axis_index("mem")
    my, mx = mem // 4, lax.rem(mem, 4)

    def peer(o):
        return lax.rem(my + o[0], 4) * 4 + lax.rem(mx + o[1], 4)

    def slot_at(o):
        return ((4 - o[0]) % 4) * 4 + (4 - o[1]) % 4

    barrier = pltpu.get_barrier_semaphore()
    for k in RING:
        pl.semaphore_signal(
            barrier, inc=1, device_id={"tp": lax.rem(tp + k, 8)}, device_id_type=MESH
        )
    for o in OFFSETS:
        pl.semaphore_signal(barrier, inc=1, device_id={"mem": peer(o)}, device_id_type=MESH)
    pl.semaphore_signal(barrier, inc=1, device_id={"section": 1 - sec}, device_id_type=MESH)
    for k in RING:
        pl.semaphore_signal(
            barrier,
            inc=1,
            device_id={"section": 1 - sec, "tp": lax.rem(tp + k, 8)},
            device_id_type=MESH,
        )

    small = [
        (owner_in, owner),
        (lengths_in, lengths),
        (hidden_in, hidden),
        (attn_gain_in, attn_gain),
        (freqs_in, freqs),
        (ffn_gain_in, ffn_gain),
    ]
    small = [pltpu.make_async_copy(s, d, ssem.at[i]) for i, (s, d) in enumerate(small)]
    for c in small:
        c.start()
    loads = [
        (w_query.at[0], wqkv.at[:, pl.ds(0, 1024)]),
        (w_key.at[0], wqkv.at[:, pl.ds(1024, 128)]),
        (w_value.at[0], wqkv.at[:, pl.ds(1152, 128)]),
        (key_cache.at[0, 0], kbuf.at[:, pl.ds(0, 128)]),
        (key_cache.at[0, 1], kbuf.at[:, pl.ds(128, 128)]),
        (value_cache.at[0, 0], vbuf.at[:, pl.ds(0, 128)]),
        (value_cache.at[0, 1], vbuf.at[:, pl.ds(128, 128)]),
        (w_out.at[0], wo),
        (w_gate.at[0], wg),
        (w_up.at[0], wu),
        (w_down.at[0], wd),
    ]
    loads = [pltpu.make_async_copy(s, d, wsem.at[i]) for i, (s, d) in enumerate(loads)]
    for c in loads:
        c.start()
    for c in small:
        c.wait()

    row = lax.broadcasted_iota(jnp.int32, (ROWS, ROWS), 0)
    col = lax.broadcasted_iota(jnp.int32, (ROWS, ROWS), 1)
    by_row = jnp.zeros((ROWS, ROWS), jnp.int32)
    by_col = jnp.zeros((ROWS, ROWS), jnp.int32)
    for j in range(ROWS):
        r = owner[j]
        by_row = jnp.where(row == j, r, by_row)
        by_col = jnp.where(col == j, r, by_col)
    to_slots = jnp.where(by_row == col, 1.0, 0.0).astype(BF16)
    to_requests = jnp.where(by_col == row, 1.0, 0.0).astype(BF16)

    len0 = lengths[owner[2 * mem]]
    len1 = lengths[owner[2 * mem + 1]]
    upper = lax.broadcasted_iota(jnp.int32, (8, 128), 0) < 4
    angles = jnp.where(upper, len0, len1).astype(F32) * freqs[...]
    cosine = jnp.cos(angles)
    sine = jnp.sin(angles)
    lane = lax.broadcasted_iota(jnp.int32, (8, 128), 1)
    sine = jnp.where(lane < 64, -sine, sine)

    across_x2 = pltpu.make_async_remote_copy(
        src_ref=x2,
        dst_ref=x2in,
        send_sem=send.at[7],
        recv_sem=recv.at[7],
        device_id={"section": 1 - sec},
        device_id_type=MESH,
    )
    across_out = pltpu.make_async_remote_copy(
        src_ref=xin,
        dst_ref=xout,
        send_sem=send.at[8],
        recv_sem=recv.at[8],
        device_id={"section": 1 - sec},
        device_id_type=MESH,
    )

    @pl.when(sec == 0)
    def _():
        xin[...] = _nn(to_slots, hidden[...]).astype(BF16)

    def summed(rb, at):
        total = rb[at].astype(F32)
        for k in range(1, 8):
            total = total + rb[at + k].astype(F32)
        return total

    @pl.when(sec == 1)
    def _():
        pl.semaphore_wait(barrier, BARRIER)
        pltpu.make_async_copy(x2, x2in, recv.at[7]).wait()
        pltpu.make_async_copy(rb6.at[pl.ds(0, 8)], rb6.at[pl.ds(0, 8)], recv6.at[0]).wait()
        xin[...] = (x2in[...].astype(F32) + summed(rb6, 0)).astype(BF16)
        across_out.start()

    x = xin[...].astype(F32)
    scaled = (x * attn_gain[...].astype(F32)).astype(BF16)
    squares = jnp.sum(x * x, axis=1, keepdims=True)
    for c in loads[:3]:
        c.wait()
    part = _nn(scaled, wqkv[...])
    for h in range(10):
        sb1[pl.ds(h, ROWS, stride=12), :] = part[:, h * 128 : (h + 1) * 128]
    sb1[pl.ds(10, ROWS, stride=12), :] = jnp.broadcast_to(squares, (ROWS, 128))
    sb1[pl.ds(11, ROWS, stride=12), :] = jnp.zeros((ROWS, 128), F32)

    @pl.when(sec == 0)
    def _():
        pl.semaphore_wait(barrier, BARRIER)

    def rows_of(m):
        return pl.ds(pl.multiple_of(m * 24, 8), 24)

    for o in OFFSETS:
        pltpu.make_async_remote_copy(
            src_ref=sb1.at[rows_of(peer(o))],
            dst_ref=rb1.at[slot_at(o)],
            send_sem=send.at[0],
            recv_sem=recv.at[0],
            device_id={"mem": peer(o)},
            device_id_type=MESH,
        ).start()
    heads = sb1[rows_of(mem), :]
    from15 = pl.ds(1, 15)
    pltpu.make_async_copy(rb1.at[from15], rb1.at[from15], recv.at[0]).wait()
    for k in range(1, 16):
        heads = heads + rb1[k]

    def turned(v, s):
        c, n = cosine[4 * s : 4 * s + 1], sine[4 * s : 4 * s + 1]
        return v * c + pltpu.roll(v, 64, 1) * n

    scale = 1.0 / math.sqrt(HD)
    zero = jnp.zeros((8, 128), F32)
    queries, owns, values = [], [], []
    for s in range(2):
        mine = heads[12 * s : 12 * s + 12]
        mine = mine * lax.rsqrt(mine[10:11] / D + EPS)
        q = turned(mine[0:8], s)
        kv = turned(mine[8:9], s).astype(BF16).astype(F32)
        values.append(jnp.broadcast_to(mine[9:10].astype(BF16).astype(F32), (8, 128)))
        q = q.astype(BF16).astype(F32)
        owns.append(jnp.sum(q * kv, axis=1, keepdims=True) * scale)
        queries.append(jnp.concatenate([q, zero] if s == 0 else [zero, q], axis=1))
    queries = jnp.concatenate(queries, axis=0).astype(BF16)
    own_score = jnp.concatenate(owns, axis=0)
    new_values = jnp.concatenate(values, axis=0)
    loads[3].wait()
    loads[4].wait()
    scores = _nt(queries, kbuf[...]) * scale
    where = lax.broadcasted_iota(jnp.int32, (16, CTX), 1)
    first = lax.broadcasted_iota(jnp.int32, (16, 1), 0) < 8
    scores = jnp.where(where < jnp.where(first, len0, len1), scores, -jnp.inf)
    peak = jnp.maximum(jnp.max(scores, axis=1, keepdims=True), own_score)
    soft = jnp.exp(scores - peak)
    own = jnp.exp(own_score - peak)
    total = jnp.sum(soft, axis=1, keepdims=True) + own
    loads[5].wait()
    loads[6].wait()
    mixed = _nn(soft.astype(BF16), vbuf[...])
    mixed = jnp.where(first, mixed[:, :128], mixed[:, 128:])
    mixed = mixed + own.astype(BF16).astype(F32) * new_values
    attended = (mixed / total).astype(BF16)
    sb2[...] = attended
    rb2[mem] = attended
    for o in OFFSETS:
        pltpu.make_async_remote_copy(
            src_ref=sb2,
            dst_ref=rb2.at[mem],
            send_sem=send.at[1],
            recv_sem=recv.at[1],
            device_id={"mem": peer(o)},
            device_id_type=MESH,
        ).start()
    loads[7].wait()
    pltpu.make_async_copy(rb2.at[from15], rb2.at[from15], recv.at[1]).wait()
    fb2[...] = rb2[...].astype(F32).reshape(256, 128)
    wide = jnp.concatenate([fb2[pl.ds(h, ROWS, stride=8), :] for h in range(8)], axis=1)
    part = _nn(wide.astype(BF16), wo[...])

    from7 = pl.ds(1, 7)

    sb3[...] = part.astype(BF16)
    for k in RING:
        pltpu.make_async_remote_copy(
            src_ref=sb3,
            dst_ref=rb3.at[tp],
            send_sem=send.at[2],
            recv_sem=recv.at[2],
            device_id={"tp": lax.rem(tp + k, 8)},
            device_id_type=MESH,
        ).start()
    rb3[tp] = sb3[...]
    pltpu.make_async_copy(rb3.at[from7], rb3.at[from7], recv.at[2]).wait()
    x = (x + summed(rb3, 0)).astype(BF16)
    x2[...] = x
    x = x.astype(F32)

    squares = jnp.sum(x * x, axis=1, keepdims=True)
    packed = jnp.zeros((8, 128), F32)
    for g in range(4):
        packed = jnp.where(lane // 32 == g, squares[8 * g : 8 * g + 8], packed)
    ssq[...] = packed
    scaled = (x * ffn_gain[...].astype(F32)).astype(BF16)
    loads[8].wait()
    loads[9].wait()

    def columns(j):
        return pl.ds(pl.multiple_of(j * 128, 128), 128)

    def units(j):
        j = jnp.minimum(j, OWNERS - 1)
        both = jnp.concatenate([wg[:, columns(j)], wu[:, columns(j)]], axis=1)
        return _nn(scaled, both)

    far_first = (OFFSETS[:5], OFFSETS[5:11], OFFSETS[11:])
    near_first = far_first[::-1]
    for group in far_first:
        for o in group:
            pltpu.make_async_remote_copy(
                src_ref=ssq,
                dst_ref=rsq.at[slot_at(o)],
                send_sem=send.at[3],
                recv_sem=recv.at[3],
                device_id={"mem": peer(o)},
                device_id_type=MESH,
            ).start()
        for o in group:
            sb4[o[0] * 4 + o[1]] = units(peer(o)).astype(BF16)
        for o in group:

            @pl.when(peer(o) < OWNERS)
            def _(o=o):
                pltpu.make_async_remote_copy(
                    src_ref=sb4.at[o[0] * 4 + o[1]],
                    dst_ref=rb4.at[slot_at(o)],
                    send_sem=send.at[4],
                    recv_sem=recv4.at[slot_at(o)],
                    device_id={"mem": peer(o)},
                    device_id_type=MESH,
                ).start()

    @pl.when(sec == 0)
    def _():
        across_x2.start()

    sums = units(mem)
    pltpu.make_async_copy(rsq.at[from15], rsq.at[from15], recv.at[3]).wait()
    for k in range(1, 16):
        packed = packed + rsq[k]
    packed = lax.rsqrt(packed / D + EPS)
    factor = jnp.concatenate([packed[:, 32 * g : 32 * g + 1] for g in range(4)], axis=0)

    @pl.when(mem < OWNERS)
    def _():
        own_units = sums
        for group in near_first:
            for k in [o[0] * 4 + o[1] for o in group]:
                pltpu.make_async_copy(rb4.at[k], rb4.at[k], recv4.at[k]).wait()
            for k in [o[0] * 4 + o[1] for o in group]:
                own_units = own_units + rb4[k].astype(F32)
        own_units = own_units * factor
        gate, up = own_units[:, :128], own_units[:, 128:]
        units_here = (gate / (1.0 + jnp.exp(-gate)) * up).astype(BF16)
        sb5[...] = units_here
        rb5[mem] = units_here
        for o in OFFSETS:
            pltpu.make_async_remote_copy(
                src_ref=sb5,
                dst_ref=rb5.at[mem],
                send_sem=send.at[5],
                recv_sem=recv5.at[slot_at(o)],
                device_id={"mem": peer(o)},
                device_id_type=MESH,
            ).start()

    @pl.when(mem >= OWNERS)
    def _():
        rb5[mem] = jnp.zeros((ROWS, 128), BF16)

    loads[10].wait()
    part = jnp.zeros((ROWS, 512), F32)
    for group in ([(0, 0)] + near_first[0],) + near_first[1:]:
        for o in group:
            if o != (0, 0):

                @pl.when(peer(o) < OWNERS)
                def _(o=o):
                    k = o[0] * 4 + o[1]
                    pltpu.make_async_copy(rb5.at[k], rb5.at[k], recv5.at[k]).wait()

                @pl.when(peer(o) >= OWNERS)
                def _(o=o):
                    rb5[peer(o)] = jnp.zeros((ROWS, 128), BF16)

        theirs = jnp.concatenate([rb5[peer(o)] for o in group], axis=1)
        down = jnp.concatenate(
            [wd[columns(jnp.minimum(peer(o), OWNERS - 1)), :] for o in group], axis=0
        )
        part = part + _nn(theirs, down)
    sb6[...] = part.astype(BF16)
    for k in RING:
        pltpu.make_async_remote_copy(
            src_ref=sb6,
            dst_ref=rb6.at[sec * 8 + tp],
            send_sem=send.at[6],
            recv_sem=recv6.at[sec],
            device_id={"section": 1, "tp": lax.rem(tp + k, 8)},
            device_id_type=MESH,
        ).start()
    across_own = pltpu.make_async_remote_copy(
        src_ref=sb6,
        dst_ref=rb6.at[tp],
        send_sem=send.at[6],
        recv_sem=recv6.at[0],
        device_id={"section": 1 - sec},
        device_id_type=MESH,
    )

    @pl.when(sec == 0)
    def _():
        across_own.start()
        pltpu.make_async_copy(xin, xout, recv.at[8]).wait()

    @pl.when(sec == 1)
    def _():
        rb6[8 + tp] = sb6[...]
        from8 = pl.ds(8, 7)
        pltpu.make_async_copy(rb6.at[from8], rb6.at[from8], recv6.at[1]).wait()
        xout[...] = (x2[...].astype(F32) + summed(rb6, 8)).astype(BF16)

    out[0] = _nn(to_requests, xout[...]).astype(BF16)

    pltpu.make_async_copy(rb1.at[from15], rb1.at[from15], send.at[0]).wait()
    pltpu.make_async_copy(rb2.at[from15], rb2.at[from15], send.at[1]).wait()
    pltpu.make_async_copy(rb3.at[from7], rb3.at[from7], send.at[2]).wait()
    pltpu.make_async_copy(rsq.at[from15], rsq.at[from15], send.at[3]).wait()

    @pl.when(mem < OWNERS)
    def _():
        from13 = pl.ds(0, 13)
        pltpu.make_async_copy(rb4.at[from13], rb4.at[from13], send.at[4]).wait()
        all15 = pl.ds(0, 15)
        pltpu.make_async_copy(rb5.at[all15], rb5.at[all15], send.at[5]).wait()

    @pl.when(mem >= OWNERS)
    def _():
        from14 = pl.ds(0, 14)
        pltpu.make_async_copy(rb4.at[from14], rb4.at[from14], send.at[4]).wait()

    @pl.when(sec == 0)
    def _():
        all8 = pl.ds(0, 8)
        pltpu.make_async_copy(rb6.at[all8], rb6.at[all8], send.at[6]).wait()
        across_x2.wait_send()

    @pl.when(sec == 1)
    def _():
        pltpu.make_async_copy(rb6.at[from7], rb6.at[from7], send.at[6]).wait()
        across_out.wait_send()


FREQS = (500000.0 ** (-(np.arange(64, dtype=np.float64) * 2.0) / 128)).astype(np.float32)
FREQS = np.concatenate([FREQS, FREQS])[None, :]


def per_device(hidden_in, lengths, owner_order, attn_gain, w_query, w_key, w_value, w_out,
               ffn_gain, w_gate, w_up, w_down, key_cache, value_cache):
    vmem = pl.BlockSpec(memory_space=pltpu.VMEM)
    hbm = pl.BlockSpec(memory_space=pl.ANY)
    V = pltpu.VMEM
    return pl.pallas_call(
        kernel,
        out_shape=pltpu.VMEM((1, ROWS, 512), BF16),
        in_specs=[hbm] * 15,
        out_specs=vmem,
        scratch_shapes=[
            pltpu.SMEM((ROWS,), jnp.int32),
            pltpu.SMEM((ROWS,), jnp.int32),
            V((1, 128), F32),
            V((ROWS, 512), BF16),
            V((1, 512), BF16),
            V((1, 512), BF16),
            V((512, 1280), BF16),
            V((1024, 512), BF16),
            V((512, 1792), BF16),
            V((512, 1792), BF16),
            V((1792, 512), BF16),
            V((CTX, 256), BF16),
            V((CTX, 256), BF16),
            V((ROWS, 512), BF16),
            V((ROWS, 512), BF16),
            V((ROWS, 512), BF16),
            V((ROWS, 512), BF16),
            V((384, 128), F32),
            V((16, 24, 128), F32),
            V((16, 128), BF16),
            V((16, 16, 128), BF16),
            V((256, 128), F32),
            V((ROWS, 512), BF16),
            V((8, ROWS, 512), BF16),
            V((8, 128), F32),
            V((16, 8, 128), F32),
            V((16, ROWS, 256), BF16),
            V((16, ROWS, 256), BF16),
            V((ROWS, 128), BF16),
            V((16, ROWS, 128), BF16),
            V((ROWS, 512), BF16),
            V((16, ROWS, 512), BF16),
            pltpu.SemaphoreType.DMA((6,)),
            pltpu.SemaphoreType.DMA((11,)),
            pltpu.SemaphoreType.DMA((9,)),
            pltpu.SemaphoreType.DMA((9,)),
            pltpu.SemaphoreType.DMA((16,)),
            pltpu.SemaphoreType.DMA((16,)),
            pltpu.SemaphoreType.DMA((2,)),
        ],
        compiler_params=pltpu.CompilerParams(
            collective_id=0, has_side_effects=True, vmem_limit_bytes=56 << 20
        ),
    )(
        lengths, owner_order, jnp.asarray(FREQS), hidden_in, attn_gain, ffn_gain,
        w_query, w_key, w_value, w_out, w_gate, w_up, w_down, key_cache, value_cache,
    )


def solution(mesh):
    placed = (
        P(None, "mem"),
        P(),
        P(),
        P("section", "mem"),
        P("section", "mem", "tp"),
        P("section", "mem", "tp"),
        P("section", "mem", "tp"),
        P("section", "tp", "mem"),
        P("section", "mem"),
        P("section", "mem", "tp"),
        P("section", "mem", "tp"),
        P("section", "tp", "mem"),
        P("section", "mem", None, "tp"),
        P("section", "mem", None, "tp"),
    )
    return jax.shard_map(
        per_device, mesh=mesh, in_specs=placed, out_specs=P("section", None, "mem"), check_vma=False
    )
```

```python
import functools
import math

import jax
import jax.numpy as jnp
import numpy as np
from jax import lax
from jax.experimental import pallas as pl
from jax.experimental.pallas import tpu as pltpu
from jax.sharding import PartitionSpec as P

D = 8192
HD = 128
CTX = 4096
ROWS = 32
EPS = 1e-05
MESH = pl.DeviceIdType.MESH
F32 = jnp.float32
BF16 = jnp.bfloat16


def _hops(o):
    return min(o[0], 4 - o[0]) + min(o[1], 4 - o[1])


OFFSETS = sorted(
    [(a, b) for a in range(4) for b in range(4) if (a, b) != (0, 0)], key=lambda o: -_hops(o)
)
RING = (4, 3, 5, 2, 6, 1, 7)
OWNERS = 14


def _nt(a, b):
    return lax.dot_general(a, b, (((1,), (1,)), ((), ())), preferred_element_type=F32)


def _nn(a, b):
    return jnp.dot(a, b, preferred_element_type=F32)


def kernel(
    lengths_in,
    owner_in,
    freqs_in,
    hidden_in,
    attn_gain_in,
    ffn_gain_in,
    w_query,
    w_key,
    w_value,
    w_out,
    w_gate,
    w_up,
    w_down,
    key_cache,
    value_cache,
    out,
    lengths,
    owner,
    freqs,
    hidden,
    attn_gain,
    ffn_gain,
    wqkv,
    kbuf,
    vbuf,
    wo,
    wg,
    wu,
    wd,
    states,
    xout,
    sb1,
    rb1,
    sb2,
    rb2,
    fb2,
    sb3,
    rb3,
    ssq,
    rsq,
    sb4,
    rb4,
    sb5,
    rb5,
    sb6,
    rb6,
    ssem,
    wsem,
    push_send,
    push_recv,
    send1,
    recv1,
    send2,
    recv2,
    send3,
    recv3,
    sendq,
    recvq,
    send4,
    recv4,
    send5,
    recv5,
    send6,
    recv6,
    sendx,
    recvx,
):
    sec = lax.axis_index("section")
    tp = lax.axis_index("tp")
    mem = lax.axis_index("mem")
    my, mx = mem // 4, lax.rem(mem, 4)

    def peer(o):
        return lax.rem(my + o[0], 4) * 4 + lax.rem(mx + o[1], 4)

    def slot_at(o):
        return ((4 - o[0]) % 4) * 4 + (4 - o[1]) % 4

    def remote(src, dst, sent, arrived, **device):
        return pltpu.make_async_remote_copy(
            src_ref=src,
            dst_ref=dst,
            send_sem=sent,
            recv_sem=arrived,
            device_id=device,
            device_id_type=MESH,
        )

    def wait_for(ref, sem):
        pltpu.make_async_copy(ref, ref, sem).wait()

    barrier = pltpu.get_barrier_semaphore()

    def greet(**device):
        pl.semaphore_signal(barrier, inc=1, device_id=device, device_id_type=MESH)

    @pl.when(sec == 0)
    def _():
        for o in OFFSETS:
            greet(mem=peer(o))
        greet(section=1)

    @pl.when(sec == 1)
    def _():
        for o in OFFSETS:
            greet(section=0, mem=peer(o))
        greet(section=0)
        for o in OFFSETS:
            greet(mem=peer(o))
        for k in RING:
            greet(tp=lax.rem(tp + k, 8))

    small = [
        (owner_in, owner),
        (lengths_in, lengths),
        (hidden_in, hidden),
        (attn_gain_in, attn_gain),
        (freqs_in, freqs),
    ]
    small = [pltpu.make_async_copy(s, d, ssem.at[i]) for i, (s, d) in enumerate(small)]
    loads = [
        (w_query.at[0], wqkv.at[:, pl.ds(0, 1024)]),
        (w_key.at[0], wqkv.at[:, pl.ds(1024, 128)]),
        (w_value.at[0], wqkv.at[:, pl.ds(1152, 128)]),
        (key_cache.at[0, 0], kbuf.at[:, pl.ds(0, 128)]),
        (key_cache.at[0, 1], kbuf.at[:, pl.ds(128, 128)]),
        (value_cache.at[0, 0], vbuf.at[:, pl.ds(0, 128)]),
        (value_cache.at[0, 1], vbuf.at[:, pl.ds(128, 128)]),
    ]
    later = [
        (w_out.at[0], wo),
        (ffn_gain_in, ffn_gain),
        (w_gate.at[0], wg),
        (w_up.at[0], wu),
        (w_down.at[0], wd),
    ]
    pushes = [
        remote(s, d.at[0], push_send.at[i], push_recv.at[i], section=1 - sec)
        for i, (s, d) in enumerate(later)
    ]
    later = [
        pltpu.make_async_copy(s, d.at[1], wsem.at[7 + i]) for i, (s, d) in enumerate(later)
    ]
    loads = [pltpu.make_async_copy(s, d, wsem.at[i]) for i, (s, d) in enumerate(loads)]
    for c in small + loads[:3]:
        c.start()
    for c in small:
        c.wait()

    row = lax.broadcasted_iota(jnp.int32, (ROWS, ROWS), 0)
    col = lax.broadcasted_iota(jnp.int32, (ROWS, ROWS), 1)
    by_row = jnp.zeros((ROWS, ROWS), jnp.int32)
    by_col = jnp.zeros((ROWS, ROWS), jnp.int32)
    for j in range(ROWS):
        r = owner[j]
        by_row = jnp.where(row == j, r, by_row)
        by_col = jnp.where(col == j, r, by_col)
    to_slots = jnp.where(by_row == col, 1.0, 0.0).astype(BF16)
    to_requests = jnp.where(by_col == row, 1.0, 0.0).astype(BF16)
    states[0] = _nn(to_slots, hidden[...]).astype(BF16)

    len0 = lengths[owner[2 * mem]]
    len1 = lengths[owner[2 * mem + 1]]
    upper = lax.broadcasted_iota(jnp.int32, (8, 128), 0) < 4
    angles = jnp.where(upper, len0, len1).astype(F32) * freqs[...]
    cosine = jnp.cos(angles)
    sine = jnp.sin(angles)
    lane = lax.broadcasted_iota(jnp.int32, (8, 128), 1)
    sine = jnp.where(lane < 64, -sine, sine)

    from15 = pl.ds(1, 15)
    from7 = pl.ds(1, 7)
    far_first = (OFFSETS[:5], OFFSETS[5:11], OFFSETS[11:])
    near_first = far_first[::-1]

    def index(o):
        return o[0] * 4 + o[1]

    def columns(j):
        return pl.ds(pl.multiple_of(j * 128, 128), 128)

    handover = remote(states.at[1], xout, sendx, recvx, section=1 - sec)

    def rest_of(layer):
        mine = rb2.at[layer]
        if layer == 0:
            wait_for(mine, recv2.at[0])
        else:
            wait_for(mine.at[from15], recv2.at[1])

        def ready(i):
            if layer == 0:
                pushes[i].wait_recv()
            else:
                later[i].wait()

        ready(0)
        fb2[...] = mine[...].astype(F32).reshape(256, 128)
        wide = jnp.concatenate([fb2[pl.ds(h, ROWS, stride=8), :] for h in range(8)], axis=1)
        part = _nn(wide.astype(BF16), wo[layer])

        def tp_sum(part, sb, rb, sent, arrived):
            sb[layer] = part.astype(BF16)
            for k in RING:
                remote(
                    sb.at[layer],
                    rb.at[layer, tp],
                    sent.at[layer],
                    arrived.at[layer],
                    tp=lax.rem(tp + k, 8),
                ).start()
            rb[layer, tp] = sb[layer]
            wait_for(rb.at[layer, from7], arrived.at[layer])
            total = rb[layer, 0].astype(F32)
            for k in range(1, 8):
                total = total + rb[layer, k].astype(F32)
            return total

        x = states[layer].astype(F32) + tp_sum(part, sb3, rb3, send3, recv3)
        x = x.astype(BF16).astype(F32)

        squares = jnp.sum(x * x, axis=1, keepdims=True)
        packed = jnp.zeros((8, 128), F32)
        for g in range(4):
            packed = jnp.where(lane // 32 == g, squares[8 * g : 8 * g + 8], packed)
        ssq[layer] = packed
        ready(1)
        scaled = (x * ffn_gain[layer].astype(F32)).astype(BF16)
        ready(2)
        ready(3)

        def units(j):
            j = jnp.minimum(j, OWNERS - 1)
            both = jnp.concatenate([wg[layer, :, columns(j)], wu[layer, :, columns(j)]], axis=1)
            return _nn(scaled, both)

        for group in far_first:
            for o in group:
                remote(
                    ssq.at[layer],
                    rsq.at[layer, slot_at(o)],
                    sendq.at[layer],
                    recvq.at[layer],
                    mem=peer(o),
                ).start()
            for o in group:
                sb4[layer, index(o)] = units(peer(o)).astype(BF16)
            for o in group:

                @pl.when(peer(o) < OWNERS)
                def _(o=o):
                    remote(
                        sb4.at[layer, index(o)],
                        rb4.at[layer, slot_at(o)],
                        send4.at[layer],
                        recv4.at[layer, slot_at(o)],
                        mem=peer(o),
                    ).start()

        sums = units(mem)
        wait_for(rsq.at[layer, from15], recvq.at[layer])
        for k in range(1, 16):
            packed = packed + rsq[layer, k]
        packed = lax.rsqrt(packed / D + EPS)
        factor = jnp.concatenate([packed[:, 32 * g : 32 * g + 1] for g in range(4)], axis=0)

        @pl.when(mem < OWNERS)
        def _():
            own_units = sums
            for group in near_first:
                for k in [index(o) for o in group]:
                    wait_for(rb4.at[layer, k], recv4.at[layer, k])
                for k in [index(o) for o in group]:
                    own_units = own_units + rb4[layer, k].astype(F32)
            own_units = own_units * factor
            gate, up = own_units[:, :128], own_units[:, 128:]
            here = (gate / (1.0 + jnp.exp(-gate)) * up).astype(BF16)
            sb5[layer] = here
            rb5[layer, mem] = here
            for o in OFFSETS:
                remote(
                    sb5.at[layer],
                    rb5.at[layer, mem],
                    send5.at[layer],
                    recv5.at[layer, slot_at(o)],
                    mem=peer(o),
                ).start()

        @pl.when(mem >= OWNERS)
        def _():
            rb5[layer, mem] = jnp.zeros((ROWS, 128), BF16)

        ready(4)
        part = jnp.zeros((ROWS, 512), F32)
        for group in ([(0, 0)] + near_first[0],) + near_first[1:]:
            for o in group:
                if o != (0, 0):

                    @pl.when(peer(o) < OWNERS)
                    def _(o=o):
                        k = index(o)
                        wait_for(rb5.at[layer, k], recv5.at[layer, k])

                    @pl.when(peer(o) >= OWNERS)
                    def _(o=o):
                        rb5[layer, peer(o)] = jnp.zeros((ROWS, 128), BF16)

            theirs = jnp.concatenate([rb5[layer, peer(o)] for o in group], axis=1)
            down = jnp.concatenate(
                [wd[layer, columns(jnp.minimum(peer(o), OWNERS - 1)), :] for o in group], axis=0
            )
            part = part + _nn(theirs, down)
        return (x + tp_sum(part, sb6, rb6, send6, recv6)).astype(BF16)

    @pl.when(sec == 1)
    def _():
        for c in loads[3:] + later:
            c.start()
        pl.semaphore_wait(barrier, 23)
        states[1] = rest_of(0)
        handover.start()

    x = states[sec].astype(F32)
    scaled = (x * attn_gain[...].astype(F32)).astype(BF16)
    squares = jnp.sum(x * x, axis=1, keepdims=True)
    for c in loads[:3]:
        c.wait()

    @pl.when(sec == 0)
    def _():
        for c in loads[3:]:
            c.start()

    part = _nn(scaled, wqkv[...])
    for h in range(10):
        sb1[pl.ds(h, ROWS, stride=12), :] = part[:, h * 128 : (h + 1) * 128]
    sb1[pl.ds(10, ROWS, stride=12), :] = jnp.broadcast_to(squares, (ROWS, 128))
    sb1[pl.ds(11, ROWS, stride=12), :] = jnp.zeros((ROWS, 128), F32)

    @pl.when(sec == 0)
    def _():
        pl.semaphore_wait(barrier, 31)

    def rows_of(m):
        return pl.ds(pl.multiple_of(m * 24, 8), 24)

    for o in OFFSETS:
        remote(
            sb1.at[rows_of(peer(o))], rb1.at[slot_at(o)], send1, recv1, mem=peer(o)
        ).start()

    @pl.when(sec == 0)
    def _():
        for c in pushes[:3]:
            c.start()

    heads = sb1[rows_of(mem), :]
    wait_for(rb1.at[from15], recv1)
    for k in range(1, 16):
        heads = heads + rb1[k]

    def turned(v, s):
        c, n = cosine[4 * s : 4 * s + 1], sine[4 * s : 4 * s + 1]
        return v * c + pltpu.roll(v, 64, 1) * n

    scale = 1.0 / math.sqrt(HD)
    zero = jnp.zeros((8, 128), F32)
    queries, owns, values = [], [], []
    for s in range(2):
        mine = heads[12 * s : 12 * s + 12]
        mine = mine * lax.rsqrt(mine[10:11] / D + EPS)
        q = turned(mine[0:8], s)
        kv = turned(mine[8:9], s).astype(BF16).astype(F32)
        values.append(jnp.broadcast_to(mine[9:10].astype(BF16).astype(F32), (8, 128)))
        q = q.astype(BF16).astype(F32)
        owns.append(jnp.sum(q * kv, axis=1, keepdims=True) * scale)
        queries.append(jnp.concatenate([q, zero] if s == 0 else [zero, q], axis=1))
    queries = jnp.concatenate(queries, axis=0).astype(BF16)
    own_score = jnp.concatenate(owns, axis=0)
    new_values = jnp.concatenate(values, axis=0)
    loads[3].wait()
    loads[4].wait()
    scores = _nt(queries, kbuf[...]) * scale
    where = lax.broadcasted_iota(jnp.int32, (16, CTX), 1)
    first = lax.broadcasted_iota(jnp.int32, (16, 1), 0) < 8
    scores = jnp.where(where < jnp.where(first, len0, len1), scores, -jnp.inf)
    peak = jnp.maximum(jnp.max(scores, axis=1, keepdims=True), own_score)
    soft = jnp.exp(scores - peak)
    own = jnp.exp(own_score - peak)
    total = jnp.sum(soft, axis=1, keepdims=True) + own
    loads[5].wait()
    loads[6].wait()
    mixed = _nn(soft.astype(BF16), vbuf[...])
    mixed = jnp.where(first, mixed[:, :128], mixed[:, 128:])
    mixed = mixed + own.astype(BF16).astype(F32) * new_values
    attended = (mixed / total).astype(BF16)
    sb2[...] = attended
    for o in OFFSETS:
        remote(sb2, rb2.at[sec, mem], send2, recv2.at[sec], section=1, mem=peer(o)).start()

    across = remote(sb2, rb2.at[0, mem], send2, recv2.at[0], section=1 - sec)

    @pl.when(sec == 0)
    def _():
        across.start()
        for c in pushes[3:]:
            c.start()
        handover.wait_recv()

    @pl.when(sec == 1)
    def _():
        rb2[1, mem] = attended
        xout[...] = rest_of(1)

    out[0] = _nn(to_requests, xout[...]).astype(BF16)

    wait_for(rb1.at[from15], send1)

    @pl.when(sec == 0)
    def _():
        wait_for(rb2.at[0], send2)
        for c in pushes:
            c.wait_send()

    @pl.when(sec == 1)
    def _():
        wait_for(rb2.at[0, from15], send2)
        handover.wait_send()
        for layer in range(2):
            wait_for(rb3.at[layer, from7], send3.at[layer])
            wait_for(rsq.at[layer, from15], sendq.at[layer])
            wait_for(rb6.at[layer, from7], send6.at[layer])

            @pl.when(mem < OWNERS)
            def _(layer=layer):
                wait_for(rb4.at[layer, pl.ds(0, 13)], send4.at[layer])
                wait_for(rb5.at[layer, pl.ds(0, 15)], send5.at[layer])

            @pl.when(mem >= OWNERS)
            def _(layer=layer):
                wait_for(rb4.at[layer, pl.ds(0, 14)], send4.at[layer])


FREQS = (500000.0 ** (-(np.arange(64, dtype=np.float64) * 2.0) / 128)).astype(np.float32)
FREQS = np.concatenate([FREQS, FREQS])[None, :]


def per_device(hidden_in, lengths, owner_order, attn_gain, w_query, w_key, w_value, w_out,
               ffn_gain, w_gate, w_up, w_down, key_cache, value_cache):
    vmem = pl.BlockSpec(memory_space=pltpu.VMEM)
    hbm = pl.BlockSpec(memory_space=pl.ANY)
    V, S = pltpu.VMEM, pltpu.SemaphoreType.DMA
    return pl.pallas_call(
        kernel,
        out_shape=pltpu.VMEM((1, ROWS, 512), BF16),
        in_specs=[hbm] * 15,
        out_specs=vmem,
        scratch_shapes=[
            pltpu.SMEM((ROWS,), jnp.int32),
            pltpu.SMEM((ROWS,), jnp.int32),
            V((1, 128), F32),
            V((ROWS, 512), BF16),
            V((1, 512), BF16),
            V((2, 1, 512), BF16),
            V((512, 1280), BF16),
            V((CTX, 256), BF16),
            V((CTX, 256), BF16),
            V((2, 1024, 512), BF16),
            V((2, 512, 1792), BF16),
            V((2, 512, 1792), BF16),
            V((2, 1792, 512), BF16),
            V((2, ROWS, 512), BF16),
            V((ROWS, 512), BF16),
            V((384, 128), F32),
            V((16, 24, 128), F32),
            V((16, 128), BF16),
            V((2, 16, 16, 128), BF16),
            V((256, 128), F32),
            V((2, ROWS, 512), BF16),
            V((2, 8, ROWS, 512), BF16),
            V((2, 8, 128), F32),
            V((2, 16, 8, 128), F32),
            V((2, 16, ROWS, 256), BF16),
            V((2, 16, ROWS, 256), BF16),
            V((2, ROWS, 128), BF16),
            V((2, 16, ROWS, 128), BF16),
            V((2, ROWS, 512), BF16),
            V((2, 8, ROWS, 512), BF16),
            S((5,)),
            S((12,)),
            S((5,)),
            S((5,)),
            S(()),
            S(()),
            S(()),
            S((2,)),
            S((2,)),
            S((2,)),
            S((2,)),
            S((2,)),
            S((2,)),
            S((2, 16)),
            S((2,)),
            S((2, 16)),
            S((2,)),
            S((2,)),
            S(()),
            S(()),
        ],
        compiler_params=pltpu.CompilerParams(
            collective_id=0, has_side_effects=True, vmem_limit_bytes=56 << 20
        ),
    )(
        lengths, owner_order, jnp.asarray(FREQS), hidden_in, attn_gain, ffn_gain,
        w_query, w_key, w_value, w_out, w_gate, w_up, w_down, key_cache, value_cache,
    )


def solution(mesh):
    placed = (
        P(None, "mem"),
        P(),
        P(),
        P("section", "mem"),
        P("section", "mem", "tp"),
        P("section", "mem", "tp"),
        P("section", "mem", "tp"),
        P("section", "tp", "mem"),
        P("section", "mem"),
        P("section", "mem", "tp"),
        P("section", "mem", "tp"),
        P("section", "tp", "mem"),
        P("section", "mem", None, "tp"),
        P("section", "mem", None, "tp"),
    )
    return jax.shard_map(
        per_device, mesh=mesh, in_specs=placed, out_specs=P("section", None, "mem"), check_vma=False
    )
```

```python
import functools
import math

import jax
import jax.numpy as jnp
import numpy as np
from jax import lax
from jax.experimental import pallas as pl
from jax.experimental.pallas import tpu as pltpu
from jax.sharding import PartitionSpec as P

D = 8192
HD = 128
CTX = 4096
ROWS = 32
EPS = 1e-05
MESH = pl.DeviceIdType.MESH
F32 = jnp.float32
BF16 = jnp.bfloat16


def _hops(o):
    return min(o[0], 4 - o[0]) + min(o[1], 4 - o[1])


OFFSETS = sorted(
    [(a, b) for a in range(4) for b in range(4) if (a, b) != (0, 0)], key=lambda o: -_hops(o)
)
RING = (4, 3, 5, 2, 6, 1, 7)
OWNERS = 14


def _nt(a, b):
    return lax.dot_general(a, b, (((1,), (1,)), ((), ())), preferred_element_type=F32)


def _nn(a, b):
    return jnp.dot(a, b, preferred_element_type=F32)


def kernel(
    lengths_in,
    owner_in,
    freqs_in,
    hidden_in,
    attn_gain_in,
    ffn_gain_in,
    w_query,
    w_key,
    w_value,
    w_out,
    w_gate,
    w_up,
    w_down,
    key_cache,
    value_cache,
    out,
    lengths,
    owner,
    freqs,
    hidden,
    attn_gain,
    ffn_gain,
    wqkv,
    kbuf,
    vbuf,
    wo,
    wg,
    wu,
    wd,
    states,
    xout,
    sw1,
    sb1,
    rb1,
    sb2,
    rb2,
    fb2,
    sb3,
    rb3,
    ssq,
    rsq,
    sb4,
    rb4,
    sb5,
    rb5,
    sb6,
    rb6,
    ssem,
    wsem,
    push_send,
    push_recv,
    send1,
    recv1,
    send2,
    recv2,
    send3,
    recv3,
    sendq,
    recvq,
    send4,
    recv4,
    send5,
    recv5,
    send6,
    recv6,
    sendx,
    recvx,
):
    sec = lax.axis_index("section")
    tp = lax.axis_index("tp")
    mem = lax.axis_index("mem")
    my, mx = mem // 4, lax.rem(mem, 4)

    def peer(o):
        return lax.rem(my + o[0], 4) * 4 + lax.rem(mx + o[1], 4)

    def slot_at(o):
        return ((4 - o[0]) % 4) * 4 + (4 - o[1]) % 4

    def remote(src, dst, sent, arrived, **device):
        return pltpu.make_async_remote_copy(
            src_ref=src,
            dst_ref=dst,
            send_sem=sent,
            recv_sem=arrived,
            device_id=device,
            device_id_type=MESH,
        )

    def wait_for(ref, sem):
        pltpu.make_async_copy(ref, ref, sem).wait()

    barrier = pltpu.get_barrier_semaphore()

    def greet(**device):
        pl.semaphore_signal(barrier, inc=1, device_id=device, device_id_type=MESH)

    @pl.when(sec == 0)
    def _():
        for o in OFFSETS:
            greet(mem=peer(o))
        greet(section=1)

    @pl.when(sec == 1)
    def _():
        for o in OFFSETS:
            greet(section=0, mem=peer(o))
        greet(section=0)
        for o in OFFSETS:
            greet(mem=peer(o))
        for k in RING:
            greet(tp=lax.rem(tp + k, 8))

    small = [
        (owner_in, owner),
        (lengths_in, lengths),
        (hidden_in, hidden),
        (attn_gain_in, attn_gain),
        (freqs_in, freqs),
    ]
    small = [pltpu.make_async_copy(s, d, ssem.at[i]) for i, (s, d) in enumerate(small)]
    loads = [
        (w_query.at[0], wqkv.at[:, pl.ds(0, 1024)]),
        (w_key.at[0], wqkv.at[:, pl.ds(1024, 128)]),
        (w_value.at[0], wqkv.at[:, pl.ds(1152, 128)]),
        (key_cache.at[0, 0], kbuf.at[0]),
        (value_cache.at[0, 0], vbuf.at[0]),
        (key_cache.at[0, 1], kbuf.at[1]),
        (value_cache.at[0, 1], vbuf.at[1]),
    ]
    later = [
        (w_out.at[0], wo),
        (ffn_gain_in, ffn_gain),
        (w_gate.at[0], wg),
        (w_up.at[0], wu),
        (w_down.at[0], wd),
    ]
    pushes = [
        remote(s, d.at[0], push_send.at[i], push_recv.at[i], section=1 - sec)
        for i, (s, d) in enumerate(later)
    ]
    later = [
        pltpu.make_async_copy(s, d.at[1], wsem.at[7 + i]) for i, (s, d) in enumerate(later)
    ]
    loads = [pltpu.make_async_copy(s, d, wsem.at[i]) for i, (s, d) in enumerate(loads)]
    for c in small + loads[:3]:
        c.start()
    for c in small:
        c.wait()

    row = lax.broadcasted_iota(jnp.int32, (ROWS, ROWS), 0)
    col = lax.broadcasted_iota(jnp.int32, (ROWS, ROWS), 1)
    by_row = jnp.zeros((ROWS, ROWS), jnp.int32)
    by_col = jnp.zeros((ROWS, ROWS), jnp.int32)
    for j in range(ROWS):
        r = owner[j]
        at = (j % 2) * 16 + j // 2
        by_row = jnp.where(row == at, r, by_row)
        by_col = jnp.where(col == at, r, by_col)
    to_slots = jnp.where(by_row == col, 1.0, 0.0).astype(BF16)
    to_requests = jnp.where(by_col == row, 1.0, 0.0).astype(BF16)
    start = _nn(to_slots, hidden[...]).astype(BF16)
    states[0] = start[:16]
    states[1] = start[16:]

    len0 = lengths[owner[2 * mem]]
    len1 = lengths[owner[2 * mem + 1]]
    upper = lax.broadcasted_iota(jnp.int32, (8, 128), 0) < 4
    angles = jnp.where(upper, len0, len1).astype(F32) * freqs[...]
    cosine = jnp.cos(angles)
    sine = jnp.sin(angles)
    lane = lax.broadcasted_iota(jnp.int32, (8, 128), 1)
    sine = jnp.where(lane < 64, -sine, sine)

    from15 = pl.ds(1, 15)
    from7 = pl.ds(1, 7)
    far_first = (OFFSETS[:5], OFFSETS[5:11], OFFSETS[11:])
    near_first = far_first[::-1]

    def index(o):
        return o[0] * 4 + o[1]

    def columns(j):
        return pl.ds(pl.multiple_of(j * 128, 128), 128)

    handovers = [
        remote(states.at[2 + h], xout.at[h], sendx.at[h], recvx.at[h], section=1 - sec)
        for h in range(2)
    ]
    lengths_here = (len0, len1)
    scale = 1.0 / math.sqrt(HD)

    def up_to_attention(layer, h):
        x = states[2 * layer + h].astype(F32)
        scaled = (x * attn_gain[...].astype(F32)).astype(BF16)
        squares = jnp.sum(x * x, axis=1, keepdims=True)
        if h == 0:
            for c in loads[:3]:
                c.wait()
            if layer == 0:
                for c in loads[3:]:
                    c.start()
        part = _nn(scaled, wqkv[...])
        wide = sw1.at[h]
        for k in range(10):
            wide[pl.ds(k, 16, stride=16), :] = part[:, k * 128 : (k + 1) * 128]
        high = squares.astype(BF16).astype(F32)
        wide[pl.ds(10, 16, stride=16), :] = jnp.broadcast_to(high, (16, 128))
        wide[pl.ds(11, 16, stride=16), :] = jnp.broadcast_to(squares - high, (16, 128))
        for k in range(12, 16):
            wide[pl.ds(k, 16, stride=16), :] = jnp.zeros((16, 128), F32)
        sb1[h] = wide[...].astype(BF16).reshape(16, 16, 128)
        if layer == 0 and h == 0:
            pl.semaphore_wait(barrier, 31)
        for o in OFFSETS:
            remote(
                sb1.at[h, peer(o)],
                rb1.at[h, slot_at(o)],
                send1.at[h],
                recv1.at[h],
                mem=peer(o),
            ).start()
        if layer == 0 and h == 1:
            for c in pushes[:3]:
                c.start()
        if layer == 1:
            handovers[h].start()
        yield

        heads = sb1[h, mem].astype(F32)
        wait_for(rb1.at[h, from15], recv1.at[h])
        for k in range(1, 16):
            heads = heads + rb1[h, k].astype(F32)
        heads = heads * lax.rsqrt((heads[10:11] + heads[11:12]) / D + EPS)
        c, n = cosine[4 * h : 4 * h + 1], sine[4 * h : 4 * h + 1]
        rotated = heads * c + pltpu.roll(heads, 64, 1) * n
        q = rotated[0:8].astype(BF16)
        new_key = rotated[8:9].astype(BF16).astype(F32)
        new_value = heads[9:10].astype(BF16).astype(F32)
        own_score = jnp.sum(q.astype(F32) * new_key, axis=1, keepdims=True) * scale
        loads[3 + 2 * h].wait()
        scores = _nt(q, kbuf[h]) * scale
        where = lax.broadcasted_iota(jnp.int32, (8, CTX), 1)
        scores = jnp.where(where < lengths_here[h], scores, -jnp.inf)
        peak = jnp.maximum(jnp.max(scores, axis=1, keepdims=True), own_score)
        soft = jnp.exp(scores - peak)
        own = jnp.exp(own_score - peak)
        total = jnp.sum(soft, axis=1, keepdims=True) + own
        loads[4 + 2 * h].wait()
        mixed = _nn(soft.astype(BF16), vbuf[h])
        mixed = mixed + own.astype(BF16).astype(F32) * new_value
        attended = (mixed / total).astype(BF16)
        sb2[h] = attended
        at = 2 * layer + h
        for o in OFFSETS:
            remote(
                sb2.at[h], rb2.at[at, mem], send2.at[h], recv2.at[at], section=1, mem=peer(o)
            ).start()
        if layer == 0:
            remote(
                sb2.at[h], rb2.at[at, mem], send2.at[h], recv2.at[at], section=1 - sec
            ).start()
            if h == 1:
                for c in pushes[3:]:
                    c.start()
        else:
            rb2[at, mem] = attended
        yield

    def rest_of(layer, h, drain=None):
        at = 2 * layer + h

        def ready(i):
            if h == 0 and layer == 0:
                pushes[i].wait_recv()
            elif h == 0:
                later[i].wait()

        def tp_send(part, sb, rb, sent, arrived):
            sb[at] = part.astype(BF16)
            for k in RING:
                remote(
                    sb.at[at], rb.at[at, tp], sent.at[at], arrived.at[at], tp=lax.rem(tp + k, 8)
                ).start()
            rb[at, tp] = sb[at]

        def tp_sum(rb, arrived):
            wait_for(rb.at[at, from7], arrived.at[at])
            total = rb[at, 0].astype(F32)
            for k in range(1, 8):
                total = total + rb[at, k].astype(F32)
            return total

        ready(0)
        if layer == 0:
            wait_for(rb2.at[at], recv2.at[at])
        else:
            wait_for(rb2.at[at, from15], recv2.at[at])
        fb2[h] = rb2[at].astype(F32).reshape(128, 128)
        wide = jnp.concatenate([fb2[h, pl.ds(k, 16, stride=8), :] for k in range(8)], axis=1)
        tp_send(_nn(wide.astype(BF16), wo[layer]), sb3, rb3, send3, recv3)
        yield

        x = states[at].astype(F32) + tp_sum(rb3, recv3)
        x = x.astype(BF16).astype(F32)

        ready(1)
        scaled = (x * ffn_gain[layer].astype(F32)).astype(BF16)
        squares = jnp.sum(x * x, axis=1, keepdims=True)
        packed = jnp.where(lane < 64, squares[0:8], squares[8:16])
        ssq[at] = packed
        ready(2)
        ready(3)

        def units(j):
            j = jnp.minimum(j, OWNERS - 1)
            both = jnp.concatenate([wg[layer, :, columns(j)], wu[layer, :, columns(j)]], axis=1)
            return _nn(scaled, both)

        for group in far_first:
            for o in group:
                sb4[at, index(o)] = units(peer(o)).astype(BF16)
            for o in group:

                @pl.when(peer(o) < OWNERS)
                def _(o=o):
                    remote(
                        sb4.at[at, index(o)],
                        rb4.at[at, slot_at(o)],
                        send4.at[at],
                        recv4.at[at, slot_at(o)],
                        mem=peer(o),
                    ).start()

            for o in group:
                remote(
                    ssq.at[at], rsq.at[at, slot_at(o)], sendq.at[at], recvq.at[at], mem=peer(o)
                ).start()
        sums = units(mem)
        yield

        @pl.when(mem < OWNERS)
        def _():
            own_units = sums
            for group in near_first:
                for k in [index(o) for o in group]:
                    wait_for(rb4.at[at, k], recv4.at[at, k])
                for k in [index(o) for o in group]:
                    own_units = own_units + rb4[at, k].astype(F32)
            wait_for(rsq.at[at, from15], recvq.at[at])
            mean = packed
            for k in range(1, 16):
                mean = mean + rsq[at, k]
            mean = lax.rsqrt(mean / D + EPS)
            factor = jnp.concatenate([mean[:, 0:1], mean[:, 64:65]], axis=0)
            own_units = own_units * factor
            gate, up = own_units[:, :128], own_units[:, 128:]
            here = (gate / (1.0 + jnp.exp(-gate)) * up).astype(BF16)
            sb5[at] = here
            rb5[at, mem] = here
            for o in OFFSETS:
                remote(
                    sb5.at[at],
                    rb5.at[at, mem],
                    send5.at[at],
                    recv5.at[at, slot_at(o)],
                    mem=peer(o),
                ).start()

        @pl.when(mem >= OWNERS)
        def _():
            wait_for(rsq.at[at, from15], recvq.at[at])
            rb5[at, mem] = jnp.zeros((16, 128), BF16)

        yield

        ready(4)
        part = jnp.zeros((16, 512), F32)
        for group in ([(0, 0)] + near_first[0],) + near_first[1:]:
            for o in group:
                if o != (0, 0):

                    @pl.when(peer(o) < OWNERS)
                    def _(o=o):
                        k = index(o)
                        wait_for(rb5.at[at, k], recv5.at[at, k])

                    @pl.when(peer(o) >= OWNERS)
                    def _(o=o):
                        rb5[at, peer(o)] = jnp.zeros((16, 128), BF16)

            theirs = jnp.concatenate([rb5[at, peer(o)] for o in group], axis=1)
            down = jnp.concatenate(
                [wd[layer, columns(jnp.minimum(peer(o), OWNERS - 1)), :] for o in group], axis=0
            )
            part = part + _nn(theirs, down)
        tp_send(part, sb6, rb6, send6, recv6)
        if drain is not None:
            drain()
        yield

        y = (x + tp_sum(rb6, recv6)).astype(BF16)
        if layer == 0:
            states[2 + h] = y
        else:
            xout[h] = y

    def side_by_side(chains):
        chains = list(chains)
        while chains:
            chains = [c for c in chains if next(c, True) is None]

    def drained():
        for h in range(2):
            wait_for(rb1.at[h, from15], send1.at[h])
            wait_for(rb2.at[h, from15], send2.at[h])
            handovers[h].wait_send()
        for at in range(4):
            wait_for(rb3.at[at, from7], send3.at[at])
            wait_for(rsq.at[at, from15], sendq.at[at])
            if at < 2:
                wait_for(rb6.at[at, from7], send6.at[at])

            @pl.when(mem < OWNERS)
            def _(at=at):
                wait_for(rb4.at[at, pl.ds(0, 13)], send4.at[at])
                wait_for(rb5.at[at, pl.ds(0, 15)], send5.at[at])

            @pl.when(mem >= OWNERS)
            def _(at=at):
                wait_for(rb4.at[at, pl.ds(0, 14)], send4.at[at])

    @pl.when(sec == 0)
    def _():
        side_by_side(up_to_attention(0, h) for h in range(2))
        for h in range(2):
            wait_for(rb1.at[h, from15], send1.at[h])
            wait_for(rb2.at[h], send2.at[h])
        for c in pushes:
            c.wait_send()
        for c in handovers:
            c.wait_recv()

    @pl.when(sec == 1)
    def _():
        for c in loads[3:] + later:
            c.start()
        pl.semaphore_wait(barrier, 23)

        def chain(h):
            yield from rest_of(0, h)
            yield from up_to_attention(1, h)
            yield from rest_of(1, h, drained if h == 1 else None)

        side_by_side(chain(h) for h in range(2))

    states_out = jnp.concatenate([xout[0], xout[1]], axis=0)
    out[0] = _nn(to_requests, states_out).astype(BF16)

    @pl.when(sec == 1)
    def _():
        for at in (2, 3):
            wait_for(rb6.at[at, from7], send6.at[at])


FREQS = (500000.0 ** (-(np.arange(64, dtype=np.float64) * 2.0) / 128)).astype(np.float32)
FREQS = np.concatenate([FREQS, FREQS])[None, :]


def per_device(hidden_in, lengths, owner_order, attn_gain, w_query, w_key, w_value, w_out,
               ffn_gain, w_gate, w_up, w_down, key_cache, value_cache):
    vmem = pl.BlockSpec(memory_space=pltpu.VMEM)
    hbm = pl.BlockSpec(memory_space=pl.ANY)
    V, S = pltpu.VMEM, pltpu.SemaphoreType.DMA
    return pl.pallas_call(
        kernel,
        out_shape=pltpu.VMEM((1, ROWS, 512), BF16),
        in_specs=[hbm] * 15,
        out_specs=vmem,
        scratch_shapes=[
            pltpu.SMEM((ROWS,), jnp.int32),
            pltpu.SMEM((ROWS,), jnp.int32),
            V((1, 128), F32),
            V((ROWS, 512), BF16),
            V((1, 512), BF16),
            V((2, 1, 512), BF16),
            V((512, 1280), BF16),
            V((2, CTX, 128), BF16),
            V((2, CTX, 128), BF16),
            V((2, 1024, 512), BF16),
            V((2, 512, 1792), BF16),
            V((2, 512, 1792), BF16),
            V((2, 1792, 512), BF16),
            V((4, 16, 512), BF16),
            V((2, 16, 512), BF16),
            V((2, 256, 128), F32),
            V((2, 16, 16, 128), BF16),
            V((2, 16, 16, 128), BF16),
            V((2, 8, 128), BF16),
            V((4, 16, 8, 128), BF16),
            V((2, 128, 128), F32),
            V((4, 16, 512), BF16),
            V((4, 8, 16, 512), BF16),
            V((4, 8, 128), F32),
            V((4, 16, 8, 128), F32),
            V((4, 16, 16, 256), BF16),
            V((4, 16, 16, 256), BF16),
            V((4, 16, 128), BF16),
            V((4, 16, 16, 128), BF16),
            V((4, 16, 512), BF16),
            V((4, 8, 16, 512), BF16),
            S((5,)),
            S((12,)),
            S((5,)),
            S((5,)),
            S((2,)),
            S((2,)),
            S((2,)),
            S((4,)),
            S((4,)),
            S((4,)),
            S((4,)),
            S((4,)),
            S((4,)),
            S((4, 16)),
            S((4,)),
            S((4, 16)),
            S((4,)),
            S((4,)),
            S((2,)),
            S((2,)),
        ],
        compiler_params=pltpu.CompilerParams(
            collective_id=0, has_side_effects=True, vmem_limit_bytes=56 << 20
        ),
    )(
        lengths, owner_order, jnp.asarray(FREQS), hidden_in, attn_gain, ffn_gain,
        w_query, w_key, w_value, w_out, w_gate, w_up, w_down, key_cache, value_cache,
    )


def solution(mesh):
    placed = (
        P(None, "mem"),
        P(),
        P(),
        P("section", "mem"),
        P("section", "mem", "tp"),
        P("section", "mem", "tp"),
        P("section", "mem", "tp"),
        P("section", "tp", "mem"),
        P("section", "mem"),
        P("section", "mem", "tp"),
        P("section", "mem", "tp"),
        P("section", "tp", "mem"),
        P("section", "mem", None, "tp"),
        P("section", "mem", None, "tp"),
    )
    return jax.shard_map(
        per_device, mesh=mesh, in_specs=placed, out_specs=P("section", None, "mem"), check_vma=False
    )
```

```python
import functools
import math

import jax
import jax.numpy as jnp
import numpy as np
from jax import lax
from jax.experimental import pallas as pl
from jax.experimental.pallas import tpu as pltpu
from jax.sharding import PartitionSpec as P

D = 8192
HD = 128
CTX = 4096
ROWS = 32
EPS = 1e-05
MESH = pl.DeviceIdType.MESH
F32 = jnp.float32
BF16 = jnp.bfloat16


def _hops(o):
    return min(o[0], 4 - o[0]) + min(o[1], 4 - o[1])


OFFSETS = sorted(
    [(a, b) for a in range(4) for b in range(4) if (a, b) != (0, 0)], key=lambda o: -_hops(o)
)
RING = (4, 3, 5, 2, 6, 1, 7)
OWNERS = 14


def _nt(a, b):
    return lax.dot_general(a, b, (((1,), (1,)), ((), ())), preferred_element_type=F32)


def _nn(a, b):
    return jnp.dot(a, b, preferred_element_type=F32)


def kernel(
    lengths_in,
    owner_in,
    freqs_in,
    hidden_in,
    attn_gain_in,
    ffn_gain_in,
    w_query,
    w_key,
    w_value,
    w_out,
    w_gate,
    w_up,
    w_down,
    key_cache,
    value_cache,
    out,
    lengths,
    owner,
    freqs,
    hidden,
    attn_gain,
    ffn_gain,
    wqkv,
    kbuf,
    vbuf,
    wo,
    wg,
    wu,
    wd,
    states,
    xout,
    sw1,
    sb1,
    rb1,
    sb2,
    rb2,
    fb2,
    sb3,
    rb3,
    ssq,
    rsq,
    sb4,
    rb4,
    sb5,
    rb5,
    sb6,
    rb6,
    ssem,
    wsem,
    push_send,
    push_recv,
    send1,
    recv1,
    send2,
    recv2,
    send3,
    recv3,
    sendq,
    recvq,
    send4,
    recv4,
    send5,
    recv5,
    send6,
    recv6,
    sendx,
    recvx,
):
    sec = lax.axis_index("section")
    tp = lax.axis_index("tp")
    mem = lax.axis_index("mem")
    my, mx = mem // 4, lax.rem(mem, 4)

    def peer(o):
        return lax.rem(my + o[0], 4) * 4 + lax.rem(mx + o[1], 4)

    def slot_at(o):
        return ((4 - o[0]) % 4) * 4 + (4 - o[1]) % 4

    def remote(src, dst, sent, arrived, **device):
        return pltpu.make_async_remote_copy(
            src_ref=src,
            dst_ref=dst,
            send_sem=sent,
            recv_sem=arrived,
            device_id=device,
            device_id_type=MESH,
        )

    def wait_for(ref, sem):
        pltpu.make_async_copy(ref, ref, sem).wait()

    barrier = pltpu.get_barrier_semaphore()

    def greet(**device):
        pl.semaphore_signal(barrier, inc=1, device_id=device, device_id_type=MESH)

    @pl.when(sec == 0)
    def _():
        for o in OFFSETS:
            greet(mem=peer(o))
        greet(section=1)

    @pl.when(sec == 1)
    def _():
        for o in OFFSETS:
            greet(section=0, mem=peer(o))
        greet(section=0)
        for o in OFFSETS:
            greet(mem=peer(o))
        for k in RING:
            greet(tp=lax.rem(tp + k, 8))

    small = [
        (owner_in, owner),
        (lengths_in, lengths),
        (hidden_in, hidden),
        (attn_gain_in, attn_gain),
        (freqs_in, freqs),
    ]
    small = [pltpu.make_async_copy(s, d, ssem.at[i]) for i, (s, d) in enumerate(small)]
    loads = [
        (w_query.at[0], wqkv.at[:, pl.ds(0, 1024)]),
        (w_key.at[0], wqkv.at[:, pl.ds(1024, 128)]),
        (w_value.at[0], wqkv.at[:, pl.ds(1152, 128)]),
        (key_cache.at[0, 0], kbuf.at[0]),
        (value_cache.at[0, 0], vbuf.at[0]),
        (key_cache.at[0, 1], kbuf.at[1]),
        (value_cache.at[0, 1], vbuf.at[1]),
    ]
    later = [
        (w_out.at[0], wo),
        (ffn_gain_in, ffn_gain),
        (w_gate.at[0], wg),
        (w_up.at[0], wu),
        (w_down.at[0], wd),
    ]
    pushes = [
        remote(s, d.at[0], push_send.at[i], push_recv.at[i], section=1 - sec)
        for i, (s, d) in enumerate(later)
    ]
    moves = [
        remote(s, d.at[2], push_send.at[5 + i], push_recv.at[5 + i], section=1 - sec)
        for i, (s, d) in enumerate([(key_cache.at[0, 0], kbuf), (value_cache.at[0, 0], vbuf)])
    ]
    later = [
        pltpu.make_async_copy(s, d.at[1], wsem.at[7 + i]) for i, (s, d) in enumerate(later)
    ]
    loads = [pltpu.make_async_copy(s, d, wsem.at[i]) for i, (s, d) in enumerate(loads)]
    for c in small + loads[:3]:
        c.start()
    for c in small:
        c.wait()

    row = lax.broadcasted_iota(jnp.int32, (ROWS, ROWS), 0)
    col = lax.broadcasted_iota(jnp.int32, (ROWS, ROWS), 1)
    by_row = jnp.zeros((ROWS, ROWS), jnp.int32)
    by_col = jnp.zeros((ROWS, ROWS), jnp.int32)
    for j in range(ROWS):
        r = owner[j]
        at = (j % 2) * 16 + j // 2
        by_row = jnp.where(row == at, r, by_row)
        by_col = jnp.where(col == at, r, by_col)
    to_slots = jnp.where(by_row == col, 1.0, 0.0).astype(BF16)
    to_requests = jnp.where(by_col == row, 1.0, 0.0).astype(BF16)
    start = _nn(to_slots, hidden[...]).astype(BF16)
    states[0] = start[:16]
    states[1] = start[16:]

    len0 = lengths[owner[2 * mem]]
    len1 = lengths[owner[2 * mem + 1]]
    upper = lax.broadcasted_iota(jnp.int32, (8, 128), 0) < 4
    angles = jnp.where(upper, len0, len1).astype(F32) * freqs[...]
    cosine = jnp.cos(angles)
    sine = jnp.sin(angles)
    lane = lax.broadcasted_iota(jnp.int32, (8, 128), 1)
    sine = jnp.where(lane < 64, -sine, sine)

    sw1[...] = jnp.zeros((2, 256, 128), F32)
    from15 = pl.ds(1, 15)
    from7 = pl.ds(1, 7)
    far_first = (OFFSETS[:5], OFFSETS[5:11], OFFSETS[11:])
    near_first = far_first[::-1]

    def index(o):
        return o[0] * 4 + o[1]

    def columns(j):
        return pl.ds(pl.multiple_of(j * 128, 128), 128)

    handovers = [
        remote(states.at[2 + h], xout.at[h], sendx.at[h], recvx.at[h], section=1 - sec)
        for h in range(2)
    ]
    lengths_here = (len0, len1)
    scale = 1.0 / math.sqrt(HD)

    def project(layer, h):
        moved = layer == 0 and h == 0
        x = states[2 * layer + h].astype(F32)
        scaled = (x * attn_gain[...].astype(F32)).astype(BF16)
        squares = jnp.sum(x * x, axis=1, keepdims=True)
        if h == 0:
            for c in loads[:3]:
                c.wait()
            if layer == 0:
                for c in loads[5:]:
                    c.start()
        part = _nn(scaled, wqkv[...])
        wide = sw1.at[h]
        for k in range(10):
            wide[pl.ds(k, 16, stride=16), :] = part[:, k * 128 : (k + 1) * 128]
        high = squares.astype(BF16).astype(F32)
        wide[pl.ds(10, 16, stride=16), :] = jnp.broadcast_to(high, (16, 128))
        wide[pl.ds(11, 16, stride=16), :] = jnp.broadcast_to(squares - high, (16, 128))
        sb1[h] = wide[...].astype(BF16).reshape(16, 16, 128)
        if layer == 0:
            yield
        if moved:
            pl.semaphore_wait(barrier, 31)
        to = 2 if moved else h
        where = {"section": 1} if moved else {}
        for o in OFFSETS:
            remote(
                sb1.at[h, peer(o)],
                rb1.at[to, slot_at(o)],
                send1.at[h],
                recv1.at[to],
                mem=peer(o),
                **where,
            ).start()
        if moved:
            remote(sb1.at[h, mem], rb1.at[2, 0], send1.at[h], recv1.at[2], section=1 - sec).start()
            for c in moves:
                c.start()
        elif layer == 0:
            for c in pushes[:2]:
                c.start()
        if layer == 1:
            handovers[h].start()
        yield

    def attend(layer, h):
        moved = layer == 0 and h == 0
        here = 2 if moved else h
        if moved:
            wait_for(rb1.at[2], recv1.at[2])
            heads = rb1[2, 0].astype(F32)
        else:
            wait_for(rb1.at[h, from15], recv1.at[h])
            heads = sb1[h, mem].astype(F32)
        for k in range(1, 16):
            heads = heads + rb1[here, k].astype(F32)
        heads = heads * lax.rsqrt((heads[10:11] + heads[11:12]) / D + EPS)
        c, n = cosine[4 * h : 4 * h + 1], sine[4 * h : 4 * h + 1]
        rotated = heads * c + pltpu.roll(heads, 64, 1) * n
        q = rotated[0:8].astype(BF16)
        new_key = rotated[8:9].astype(BF16).astype(F32)
        new_value = heads[9:10].astype(BF16).astype(F32)
        own_score = jnp.sum(q.astype(F32) * new_key, axis=1, keepdims=True) * scale
        if moved:
            moves[0].wait_recv()
        else:
            loads[3 + 2 * h].wait()
        scores = _nt(q, kbuf[here]) * scale
        where = lax.broadcasted_iota(jnp.int32, (8, CTX), 1)
        scores = jnp.where(where < lengths_here[h], scores, -jnp.inf)
        peak = jnp.maximum(jnp.max(scores, axis=1, keepdims=True), own_score)
        soft = jnp.exp(scores - peak)
        own = jnp.exp(own_score - peak)
        total = jnp.sum(soft, axis=1, keepdims=True) + own
        if moved:
            moves[1].wait_recv()
        else:
            loads[4 + 2 * h].wait()
        mixed = _nn(soft.astype(BF16), vbuf[here])
        mixed = mixed + own.astype(BF16).astype(F32) * new_value
        attended = (mixed / total).astype(BF16)
        sb2[here] = attended
        at = 2 * layer + h
        for o in OFFSETS:
            remote(
                sb2.at[here], rb2.at[at, mem], send2.at[here], recv2.at[at], section=1, mem=peer(o)
            ).start()
        if layer == 0 and not moved:
            remote(
                sb2.at[h], rb2.at[at, mem], send2.at[h], recv2.at[at], section=1 - sec
            ).start()
            for c in pushes[2:]:
                c.start()
        else:
            rb2[at, mem] = attended
        yield

    def rest_of(layer, h, drain=None):
        at = 2 * layer + h

        def ready(i):
            if h == 0 and layer == 0:
                pushes[i].wait_recv()
            elif h == 0:
                later[i].wait()

        def tp_send(part, sb, rb, sent, arrived):
            sb[at] = part.astype(BF16)
            for k in RING:
                remote(
                    sb.at[at], rb.at[at, tp], sent.at[at], arrived.at[at], tp=lax.rem(tp + k, 8)
                ).start()
            rb[at, tp] = sb[at]

        def tp_sum(rb, arrived):
            wait_for(rb.at[at, from7], arrived.at[at])
            total = rb[at, 0].astype(F32)
            for k in range(1, 8):
                total = total + rb[at, k].astype(F32)
            return total

        ready(0)
        if layer == 0 and h == 1:
            wait_for(rb2.at[at], recv2.at[at])
        else:
            wait_for(rb2.at[at, from15], recv2.at[at])
        fb2[h] = rb2[at].astype(F32).reshape(128, 128)
        wide = jnp.concatenate([fb2[h, pl.ds(k, 16, stride=8), :] for k in range(8)], axis=1)
        tp_send(_nn(wide.astype(BF16), wo[layer]), sb3, rb3, send3, recv3)
        yield

        x = states[at].astype(F32) + tp_sum(rb3, recv3)
        x = x.astype(BF16).astype(F32)

        ready(1)
        scaled = (x * ffn_gain[layer].astype(F32)).astype(BF16)
        squares = jnp.sum(x * x, axis=1, keepdims=True)
        packed = jnp.where(lane < 64, squares[0:8], squares[8:16])
        ssq[at] = packed
        ready(2)
        ready(3)

        def units(j):
            j = jnp.minimum(j, OWNERS - 1)
            both = jnp.concatenate([wg[layer, :, columns(j)], wu[layer, :, columns(j)]], axis=1)
            return _nn(scaled, both)

        for group in far_first:
            for o in group:
                sb4[at, index(o)] = units(peer(o)).astype(BF16)
            for o in group:

                @pl.when(peer(o) < OWNERS)
                def _(o=o):
                    remote(
                        sb4.at[at, index(o)],
                        rb4.at[at, slot_at(o)],
                        send4.at[at],
                        recv4.at[at, slot_at(o)],
                        mem=peer(o),
                    ).start()

            for o in group:
                remote(
                    ssq.at[at], rsq.at[at, slot_at(o)], sendq.at[at], recvq.at[at], mem=peer(o)
                ).start()
        sums = units(mem)
        yield

        @pl.when(mem < OWNERS)
        def _():
            own_units = sums
            for group in near_first:
                for k in [index(o) for o in group]:
                    wait_for(rb4.at[at, k], recv4.at[at, k])
                for k in [index(o) for o in group]:
                    own_units = own_units + rb4[at, k].astype(F32)
            wait_for(rsq.at[at, from15], recvq.at[at])
            mean = packed
            for k in range(1, 16):
                mean = mean + rsq[at, k]
            mean = lax.rsqrt(mean / D + EPS)
            factor = jnp.concatenate([mean[:, 0:1], mean[:, 64:65]], axis=0)
            own_units = own_units * factor
            gate, up = own_units[:, :128], own_units[:, 128:]
            here = (gate / (1.0 + jnp.exp(-gate)) * up).astype(BF16)
            sb5[at] = here
            rb5[at, mem] = here
            for o in OFFSETS:
                remote(
                    sb5.at[at],
                    rb5.at[at, mem],
                    send5.at[at],
                    recv5.at[at, slot_at(o)],
                    mem=peer(o),
                ).start()

        @pl.when(mem >= OWNERS)
        def _():
            wait_for(rsq.at[at, from15], recvq.at[at])
            rb5[at, mem] = jnp.zeros((16, 128), BF16)

        yield

        ready(4)
        part = jnp.zeros((16, 512), F32)
        for group in ([(0, 0)] + near_first[0],) + near_first[1:]:
            for o in group:
                if o != (0, 0):

                    @pl.when(peer(o) < OWNERS)
                    def _(o=o):
                        k = index(o)
                        wait_for(rb5.at[at, k], recv5.at[at, k])

                    @pl.when(peer(o) >= OWNERS)
                    def _(o=o):
                        rb5[at, peer(o)] = jnp.zeros((16, 128), BF16)

            theirs = jnp.concatenate([rb5[at, peer(o)] for o in group], axis=1)
            down = jnp.concatenate(
                [wd[layer, columns(jnp.minimum(peer(o), OWNERS - 1)), :] for o in group], axis=0
            )
            part = part + _nn(theirs, down)
        tp_send(part, sb6, rb6, send6, recv6)
        if drain is not None:
            drain()
        yield

        y = (x + tp_sum(rb6, recv6)).astype(BF16)
        if layer == 0:
            states[2 + h] = y
        else:
            xout[h] = y

    def side_by_side(chains):
        chains = list(chains)
        while chains:
            chains = [c for c in chains if next(c, True) is None]

    def drained():
        for h in range(2):
            wait_for(rb1.at[h, from15], send1.at[h])
            handovers[h].wait_send()
        for k in range(3):
            wait_for(rb2.at[k, from15], send2.at[k])
        for at in range(4):
            wait_for(rb3.at[at, from7], send3.at[at])
            wait_for(rsq.at[at, from15], sendq.at[at])
            if at < 2:
                wait_for(rb6.at[at, from7], send6.at[at])

            @pl.when(mem < OWNERS)
            def _(at=at):
                wait_for(rb4.at[at, pl.ds(0, 13)], send4.at[at])
                wait_for(rb5.at[at, pl.ds(0, 15)], send5.at[at])

            @pl.when(mem >= OWNERS)
            def _(at=at):
                wait_for(rb4.at[at, pl.ds(0, 14)], send4.at[at])

    @pl.when(sec == 0)
    def _():
        def half1():
            yield from project(0, 1)
            yield from attend(0, 1)

        side_by_side([project(0, 0), half1()])
        wait_for(rb1.at[0], send1.at[0])
        wait_for(rb1.at[0, from15], send1.at[1])
        wait_for(rb2.at[0], send2.at[1])
        for c in moves + pushes:
            c.wait_send()
        for c in handovers:
            c.wait_recv()

    @pl.when(sec == 1)
    def _():
        for c in loads[3:] + later:
            c.start()
        pl.semaphore_wait(barrier, 23)

        def chain(h):
            if h == 0:
                yield from attend(0, 0)
            else:
                yield
            yield from rest_of(0, h)
            yield from project(1, h)
            yield from attend(1, h)
            yield from rest_of(1, h, drained if h == 1 else None)

        side_by_side(chain(h) for h in range(2))

    states_out = jnp.concatenate([xout[0], xout[1]], axis=0)
    out[0] = _nn(to_requests, states_out).astype(BF16)

    @pl.when(sec == 1)
    def _():
        for at in (2, 3):
            wait_for(rb6.at[at, from7], send6.at[at])


FREQS = (500000.0 ** (-(np.arange(64, dtype=np.float64) * 2.0) / 128)).astype(np.float32)
FREQS = np.concatenate([FREQS, FREQS])[None, :]


def per_device(hidden_in, lengths, owner_order, attn_gain, w_query, w_key, w_value, w_out,
               ffn_gain, w_gate, w_up, w_down, key_cache, value_cache):
    vmem = pl.BlockSpec(memory_space=pltpu.VMEM)
    hbm = pl.BlockSpec(memory_space=pl.ANY)
    V, S = pltpu.VMEM, pltpu.SemaphoreType.DMA
    return pl.pallas_call(
        kernel,
        out_shape=pltpu.VMEM((1, ROWS, 512), BF16),
        in_specs=[hbm] * 15,
        out_specs=vmem,
        scratch_shapes=[
            pltpu.SMEM((ROWS,), jnp.int32),
            pltpu.SMEM((ROWS,), jnp.int32),
            V((1, 128), F32),
            V((ROWS, 512), BF16),
            V((1, 512), BF16),
            V((2, 1, 512), BF16),
            V((512, 1280), BF16),
            V((3, CTX, 128), BF16),
            V((3, CTX, 128), BF16),
            V((2, 1024, 512), BF16),
            V((2, 512, 1792), BF16),
            V((2, 512, 1792), BF16),
            V((2, 1792, 512), BF16),
            V((4, 16, 512), BF16),
            V((2, 16, 512), BF16),
            V((2, 256, 128), F32),
            V((2, 16, 16, 128), BF16),
            V((3, 16, 16, 128), BF16),
            V((3, 8, 128), BF16),
            V((4, 16, 8, 128), BF16),
            V((2, 128, 128), F32),
            V((4, 16, 512), BF16),
            V((4, 8, 16, 512), BF16),
            V((4, 8, 128), F32),
            V((4, 16, 8, 128), F32),
            V((4, 16, 16, 256), BF16),
            V((4, 16, 16, 256), BF16),
            V((4, 16, 128), BF16),
            V((4, 16, 16, 128), BF16),
            V((4, 16, 512), BF16),
            V((4, 8, 16, 512), BF16),
            S((5,)),
            S((12,)),
            S((7,)),
            S((7,)),
            S((2,)),
            S((3,)),
            S((3,)),
            S((4,)),
            S((4,)),
            S((4,)),
            S((4,)),
            S((4,)),
            S((4,)),
            S((4, 16)),
            S((4,)),
            S((4, 16)),
            S((4,)),
            S((4,)),
            S((2,)),
            S((2,)),
        ],
        compiler_params=pltpu.CompilerParams(
            collective_id=0, has_side_effects=True, vmem_limit_bytes=56 << 20
        ),
    )(
        lengths, owner_order, jnp.asarray(FREQS), hidden_in, attn_gain, ffn_gain,
        w_query, w_key, w_value, w_out, w_gate, w_up, w_down, key_cache, value_cache,
    )


def solution(mesh):
    placed = (
        P(None, "mem"),
        P(),
        P(),
        P("section", "mem"),
        P("section", "mem", "tp"),
        P("section", "mem", "tp"),
        P("section", "mem", "tp"),
        P("section", "tp", "mem"),
        P("section", "mem"),
        P("section", "mem", "tp"),
        P("section", "mem", "tp"),
        P("section", "tp", "mem"),
        P("section", "mem", None, "tp"),
        P("section", "mem", None, "tp"),
    )
    return jax.shard_map(
        per_device, mesh=mesh, in_specs=placed, out_specs=P("section", None, "mem"), check_vma=False
    )
```

```python
import functools
import math

import jax
import jax.numpy as jnp
import numpy as np
from jax import lax
from jax.experimental import pallas as pl
from jax.experimental.pallas import tpu as pltpu
from jax.sharding import PartitionSpec as P

D = 8192
HD = 128
CTX = 4096
ROWS = 32
EPS = 1e-05
MESH = pl.DeviceIdType.MESH
F32 = jnp.float32
BF16 = jnp.bfloat16


def _hops(o):
    return min(o[0], 4 - o[0]) + min(o[1], 4 - o[1])


OFFSETS = sorted(
    [(a, b) for a in range(4) for b in range(4) if (a, b) != (0, 0)], key=lambda o: -_hops(o)
)
RING = (4, 3, 5, 2, 6, 1, 7)
OWNERS = 14


def _nt(a, b):
    return lax.dot_general(a, b, (((1,), (1,)), ((), ())), preferred_element_type=F32)


def _nn(a, b):
    return jnp.dot(a, b, preferred_element_type=F32)


def kernel(
    lengths_in,
    owner_in,
    freqs_in,
    hidden_in,
    attn_gain_in,
    ffn_gain_in,
    w_query,
    w_key,
    w_value,
    w_out,
    w_gate,
    w_up,
    w_down,
    key_cache,
    value_cache,
    out,
    lengths,
    owner,
    freqs,
    hidden,
    attn_gain,
    ffn_gain,
    wqkv,
    kbuf,
    vbuf,
    wo,
    wg,
    wu,
    wd,
    states,
    xout,
    sw1,
    sb1,
    rb1,
    sb2,
    rb2,
    fb2,
    sb3,
    rb3,
    ssq,
    rsq,
    sb4,
    rb4,
    sb5,
    rb5,
    sb6,
    rb6,
    ssem,
    wsem,
    push_send,
    push_recv,
    send1,
    recv1,
    send2,
    recv2,
    send3,
    recv3,
    sendq,
    recvq,
    send4,
    recv4,
    send5,
    recv5,
    send6,
    recv6,
    sendx,
    recvx,
):
    sec = lax.axis_index("section")
    tp = lax.axis_index("tp")
    mem = lax.axis_index("mem")
    my, mx = mem // 4, lax.rem(mem, 4)

    def peer(o):
        return lax.rem(my + o[0], 4) * 4 + lax.rem(mx + o[1], 4)

    peers = {o: peer(o) for o in [(0, 0)] + OFFSETS}
    ring = {k: lax.rem(tp + k, 8) for k in RING}

    def peer(o):
        return peers[o]

    def slot_at(o):
        return ((4 - o[0]) % 4) * 4 + (4 - o[1]) % 4

    def remote(src, dst, sent, arrived, **device):
        return pltpu.make_async_remote_copy(
            src_ref=src,
            dst_ref=dst,
            send_sem=sent,
            recv_sem=arrived,
            device_id=device,
            device_id_type=MESH,
        )

    def wait_for(ref, sem):
        pltpu.make_async_copy(ref, ref, sem).wait()

    barrier = pltpu.get_barrier_semaphore()

    def greet(**device):
        pl.semaphore_signal(barrier, inc=1, device_id=device, device_id_type=MESH)

    @pl.when(sec == 0)
    def _():
        for o in OFFSETS:
            greet(mem=peer(o))
        greet(section=1)

    @pl.when(sec == 1)
    def _():
        for o in OFFSETS:
            greet(section=0, mem=peer(o))
        greet(section=0)
        for o in OFFSETS:
            greet(mem=peer(o))
        for k in RING:
            greet(tp=lax.rem(tp + k, 8))

    small = [
        (owner_in, owner),
        (lengths_in, lengths),
        (hidden_in, hidden),
        (attn_gain_in, attn_gain),
        (freqs_in, freqs),
    ]
    small = [pltpu.make_async_copy(s, d, ssem.at[i]) for i, (s, d) in enumerate(small)]
    loads = [
        (w_query.at[0], wqkv.at[:, pl.ds(0, 1024)]),
        (w_key.at[0], wqkv.at[:, pl.ds(1024, 128)]),
        (w_value.at[0], wqkv.at[:, pl.ds(1152, 128)]),
        (key_cache.at[0, 0], kbuf.at[0]),
        (value_cache.at[0, 0], vbuf.at[0]),
        (key_cache.at[0, 1], kbuf.at[1]),
        (value_cache.at[0, 1], vbuf.at[1]),
    ]
    later = [
        (w_out.at[0], wo),
        (ffn_gain_in, ffn_gain),
        (w_gate.at[0], wg),
        (w_up.at[0], wu),
        (w_down.at[0], wd),
    ]
    pushes = [
        remote(s, d.at[0], push_send.at[i], push_recv.at[i], section=1 - sec)
        for i, (s, d) in enumerate(later)
    ]
    moves = [
        remote(s, d.at[2], push_send.at[5 + i], push_recv.at[5 + i], section=1 - sec)
        for i, (s, d) in enumerate([(key_cache.at[0, 0], kbuf), (value_cache.at[0, 0], vbuf)])
    ]
    later = [
        pltpu.make_async_copy(s, d.at[1], wsem.at[7 + i]) for i, (s, d) in enumerate(later)
    ]
    loads = [pltpu.make_async_copy(s, d, wsem.at[i]) for i, (s, d) in enumerate(loads)]
    for c in small + loads[:3]:
        c.start()
    for c in small:
        c.wait()

    row = lax.broadcasted_iota(jnp.int32, (ROWS, ROWS), 0)
    col = lax.broadcasted_iota(jnp.int32, (ROWS, ROWS), 1)
    by_row = jnp.zeros((ROWS, ROWS), jnp.int32)
    by_col = jnp.zeros((ROWS, ROWS), jnp.int32)
    for j in range(ROWS):
        r = owner[j]
        at = (j % 2) * 16 + j // 2
        by_row = jnp.where(row == at, r, by_row)
        by_col = jnp.where(col == at, r, by_col)
    to_slots = jnp.where(by_row == col, 1.0, 0.0).astype(BF16)
    to_requests = jnp.where(by_col == row, 1.0, 0.0).astype(BF16)
    start = _nn(to_slots, hidden[...]).astype(BF16)
    states[0] = start[:16]
    states[1] = start[16:]

    len0 = lengths[owner[2 * mem]]
    len1 = lengths[owner[2 * mem + 1]]
    upper = lax.broadcasted_iota(jnp.int32, (8, 128), 0) < 4
    angles = jnp.where(upper, len0, len1).astype(F32) * freqs[...]
    cosine = jnp.cos(angles)
    sine = jnp.sin(angles)
    lane = lax.broadcasted_iota(jnp.int32, (8, 128), 1)
    sine = jnp.where(lane < 64, -sine, sine)

    sw1[...] = jnp.zeros((2, 256, 128), F32)
    from15 = pl.ds(1, 15)
    from7 = pl.ds(1, 7)
    far_first = (OFFSETS[:1], OFFSETS[1:5], OFFSETS[5:11], OFFSETS[11:])
    near_first = far_first[::-1]

    def index(o):
        return o[0] * 4 + o[1]

    def columns(j):
        return pl.ds(pl.multiple_of(j * 128, 128), 128)

    handovers = [
        remote(states.at[2 + h], xout.at[h], sendx.at[h], recvx.at[h], section=1 - sec)
        for h in range(2)
    ]
    lengths_here = (len0, len1)
    scale = 1.0 / math.sqrt(HD)

    def project(layer, h):
        moved = layer == 0 and h == 0
        x = states[2 * layer + h].astype(F32)
        scaled = (x * attn_gain[...].astype(F32)).astype(BF16)
        squares = jnp.sum(x * x, axis=1, keepdims=True)
        if h == 0:
            for c in loads[:3]:
                c.wait()
            if layer == 0:
                for c in loads[5:]:
                    c.start()
        part = _nn(scaled, wqkv[...])
        wide = sw1.at[h]
        for k in range(10):
            wide[pl.ds(k, 16, stride=16), :] = part[:, k * 128 : (k + 1) * 128]
        high = squares.astype(BF16).astype(F32)
        wide[pl.ds(10, 16, stride=16), :] = jnp.broadcast_to(high, (16, 128))
        wide[pl.ds(11, 16, stride=16), :] = jnp.broadcast_to(squares - high, (16, 128))
        sb1[h] = wide[...].astype(BF16).reshape(16, 16, 128)
        if layer == 0:
            yield
        if moved:
            pl.semaphore_wait(barrier, 31)
        to = 2 if moved else h
        where = {"section": 1} if moved else {}
        for o in OFFSETS:
            remote(
                sb1.at[h, peer(o)],
                rb1.at[to, slot_at(o)],
                send1.at[h],
                recv1.at[to],
                mem=peer(o),
                **where,
            ).start()
        if moved:
            remote(sb1.at[h, mem], rb1.at[2, 0], send1.at[h], recv1.at[2], section=1 - sec).start()
            for c in moves:
                c.start()
        elif layer == 0:
            for c in pushes[:2]:
                c.start()
        if layer == 1:
            handovers[h].start()
        yield

    def attend(layer, h):
        moved = layer == 0 and h == 0
        here = 2 if moved else h
        if moved:
            wait_for(rb1.at[2], recv1.at[2])
            heads = rb1[2, 0].astype(F32)
        else:
            wait_for(rb1.at[h, from15], recv1.at[h])
            heads = sb1[h, mem].astype(F32)
        for k in range(1, 16):
            heads = heads + rb1[here, k].astype(F32)
        heads = heads * lax.rsqrt((heads[10:11] + heads[11:12]) / D + EPS)
        c, n = cosine[4 * h : 4 * h + 1], sine[4 * h : 4 * h + 1]
        rotated = heads * c + pltpu.roll(heads, 64, 1) * n
        q = rotated[0:8].astype(BF16)
        new_key = rotated[8:9].astype(BF16).astype(F32)
        new_value = heads[9:10].astype(BF16).astype(F32)
        own_score = jnp.sum(q.astype(F32) * new_key, axis=1, keepdims=True) * scale
        if moved:
            moves[0].wait_recv()
        else:
            loads[3 + 2 * h].wait()
        scores = _nt(q, kbuf[here]) * scale
        where = lax.broadcasted_iota(jnp.int32, (8, CTX), 1)
        scores = jnp.where(where < lengths_here[h], scores, -jnp.inf)
        peak = jnp.maximum(jnp.max(scores, axis=1, keepdims=True), own_score)
        soft = jnp.exp(scores - peak)
        own = jnp.exp(own_score - peak)
        total = jnp.sum(soft, axis=1, keepdims=True) + own
        if moved:
            moves[1].wait_recv()
        else:
            loads[4 + 2 * h].wait()
        mixed = _nn(soft.astype(BF16), vbuf[here])
        mixed = mixed + own.astype(BF16).astype(F32) * new_value
        attended = (mixed / total).astype(BF16)
        sb2[here] = attended
        at = 2 * layer + h
        for o in OFFSETS:
            remote(
                sb2.at[here], rb2.at[at, mem], send2.at[here], recv2.at[at], section=1, mem=peer(o)
            ).start()
        if layer == 0 and not moved:
            remote(
                sb2.at[h], rb2.at[at, mem], send2.at[h], recv2.at[at], section=1 - sec
            ).start()
            for c in pushes[2:]:
                c.start()
        else:
            rb2[at, mem] = attended
        yield

    def rest_of(layer, h, drain=None):
        at = 2 * layer + h

        def ready(i):
            if h == 0 and layer == 0:
                pushes[i].wait_recv()
            elif h == 0:
                later[i].wait()

        def tp_send(part, sb, rb, sent, arrived):
            sb[at] = part.astype(BF16)
            for k in RING:
                remote(
                    sb.at[at], rb.at[at, tp], sent.at[at], arrived.at[at], tp=ring[k]
                ).start()
            rb[at, tp] = sb[at]

        def tp_sum(rb, arrived):
            wait_for(rb.at[at, from7], arrived.at[at])
            total = rb[at, 0].astype(F32)
            for k in range(1, 8):
                total = total + rb[at, k].astype(F32)
            return total

        ready(0)
        if layer == 0 and h == 1:
            wait_for(rb2.at[at], recv2.at[at])
        else:
            wait_for(rb2.at[at, from15], recv2.at[at])
        fb2[h] = rb2[at].astype(F32).reshape(128, 128)
        wide = jnp.concatenate([fb2[h, pl.ds(k, 16, stride=8), :] for k in range(8)], axis=1)
        tp_send(_nn(wide.astype(BF16), wo[layer]), sb3, rb3, send3, recv3)
        yield

        x = states[at].astype(F32) + tp_sum(rb3, recv3)
        x = x.astype(BF16).astype(F32)

        ready(1)
        scaled = (x * ffn_gain[layer].astype(F32)).astype(BF16)
        squares = jnp.sum(x * x, axis=1, keepdims=True)
        packed = jnp.where(lane < 64, squares[0:8], squares[8:16])
        ssq[at] = packed
        ready(2)
        ready(3)

        def units(j):
            j = jnp.minimum(j, OWNERS - 1)
            both = jnp.concatenate([wg[layer, :, columns(j)], wu[layer, :, columns(j)]], axis=1)
            return _nn(scaled, both)

        for group in far_first:
            for o in group:
                sb4[at, index(o)] = units(peer(o)).astype(BF16)
            for o in group:

                @pl.when(peer(o) < OWNERS)
                def _(o=o):
                    remote(
                        sb4.at[at, index(o)],
                        rb4.at[at, slot_at(o)],
                        send4.at[at],
                        recv4.at[at, slot_at(o)],
                        mem=peer(o),
                    ).start()

            for o in group:
                remote(
                    ssq.at[at], rsq.at[at, slot_at(o)], sendq.at[at], recvq.at[at], mem=peer(o)
                ).start()
        sums = units(mem)
        yield

        @pl.when(mem < OWNERS)
        def _():
            own_units = sums
            for group in near_first:
                for k in [index(o) for o in group]:
                    wait_for(rb4.at[at, k], recv4.at[at, k])
                for k in [index(o) for o in group]:
                    own_units = own_units + rb4[at, k].astype(F32)
            wait_for(rsq.at[at, from15], recvq.at[at])
            mean = packed
            for k in range(1, 16):
                mean = mean + rsq[at, k]
            mean = lax.rsqrt(mean / D + EPS)
            factor = jnp.concatenate([mean[:, 0:1], mean[:, 64:65]], axis=0)
            own_units = own_units * factor
            gate, up = own_units[:, :128], own_units[:, 128:]
            here = (gate / (1.0 + jnp.exp(-gate)) * up).astype(BF16)
            sb5[at] = here
            rb5[at, mem] = here
            for o in OFFSETS:
                remote(
                    sb5.at[at],
                    rb5.at[at, mem],
                    send5.at[at],
                    recv5.at[at, slot_at(o)],
                    mem=peer(o),
                ).start()

        @pl.when(mem >= OWNERS)
        def _():
            wait_for(rsq.at[at, from15], recvq.at[at])
            rb5[at, mem] = jnp.zeros((16, 128), BF16)

        yield

        ready(4)
        part = jnp.zeros((16, 512), F32)
        for group in ([(0, 0)] + near_first[0],) + near_first[1:]:
            for o in group:
                if o != (0, 0):

                    @pl.when(peer(o) < OWNERS)
                    def _(o=o):
                        k = index(o)
                        wait_for(rb5.at[at, k], recv5.at[at, k])

                    @pl.when(peer(o) >= OWNERS)
                    def _(o=o):
                        rb5[at, peer(o)] = jnp.zeros((16, 128), BF16)

            theirs = jnp.concatenate([rb5[at, peer(o)] for o in group], axis=1)
            down = jnp.concatenate(
                [wd[layer, columns(jnp.minimum(peer(o), OWNERS - 1)), :] for o in group], axis=0
            )
            part = part + _nn(theirs, down)
        tp_send(part, sb6, rb6, send6, recv6)
        if drain is not None:
            drain()
        yield

        y = (x + tp_sum(rb6, recv6)).astype(BF16)
        if layer == 0:
            states[2 + h] = y
        else:
            xout[h] = y

    def side_by_side(chains):
        chains = list(chains)
        while chains:
            chains = [c for c in chains if next(c, True) is None]

    def drained():
        for h in range(2):
            wait_for(rb1.at[h, from15], send1.at[h])
            handovers[h].wait_send()
        for k in range(3):
            wait_for(rb2.at[k, from15], send2.at[k])
        for at in range(4):
            wait_for(rb3.at[at, from7], send3.at[at])
            wait_for(rsq.at[at, from15], sendq.at[at])
            if at < 2:
                wait_for(rb6.at[at, from7], send6.at[at])

            @pl.when(mem < OWNERS)
            def _(at=at):
                wait_for(rb4.at[at, pl.ds(0, 13)], send4.at[at])
                wait_for(rb5.at[at, pl.ds(0, 15)], send5.at[at])

            @pl.when(mem >= OWNERS)
            def _(at=at):
                wait_for(rb4.at[at, pl.ds(0, 14)], send4.at[at])

    @pl.when(sec == 0)
    def _():
        def half1():
            yield from project(0, 1)
            yield from attend(0, 1)

        side_by_side([project(0, 0), half1()])
        wait_for(rb1.at[0], send1.at[0])
        wait_for(rb1.at[0, from15], send1.at[1])
        wait_for(rb2.at[0], send2.at[1])
        for c in moves + pushes:
            c.wait_send()
        for c in handovers:
            c.wait_recv()

    @pl.when(sec == 1)
    def _():
        for c in loads[3:] + later:
            c.start()
        pl.semaphore_wait(barrier, 23)

        def chain(h):
            if h == 0:
                yield from attend(0, 0)
            else:
                yield
            yield from rest_of(0, h)
            yield from project(1, h)
            yield from attend(1, h)
            yield from rest_of(1, h, drained if h == 1 else None)

        side_by_side(chain(h) for h in range(2))

    states_out = jnp.concatenate([xout[0], xout[1]], axis=0)
    out[0] = _nn(to_requests, states_out).astype(BF16)

    @pl.when(sec == 1)
    def _():
        for at in (2, 3):
            wait_for(rb6.at[at, from7], send6.at[at])


FREQS = (500000.0 ** (-(np.arange(64, dtype=np.float64) * 2.0) / 128)).astype(np.float32)
FREQS = np.concatenate([FREQS, FREQS])[None, :]


def per_device(hidden_in, lengths, owner_order, attn_gain, w_query, w_key, w_value, w_out,
               ffn_gain, w_gate, w_up, w_down, key_cache, value_cache):
    vmem = pl.BlockSpec(memory_space=pltpu.VMEM)
    hbm = pl.BlockSpec(memory_space=pl.ANY)
    V, S = pltpu.VMEM, pltpu.SemaphoreType.DMA
    return pl.pallas_call(
        kernel,
        out_shape=pltpu.VMEM((1, ROWS, 512), BF16),
        in_specs=[hbm] * 15,
        out_specs=vmem,
        scratch_shapes=[
            pltpu.SMEM((ROWS,), jnp.int32),
            pltpu.SMEM((ROWS,), jnp.int32),
            V((1, 128), F32),
            V((ROWS, 512), BF16),
            V((1, 512), BF16),
            V((2, 1, 512), BF16),
            V((512, 1280), BF16),
            V((3, CTX, 128), BF16),
            V((3, CTX, 128), BF16),
            V((2, 1024, 512), BF16),
            V((2, 512, 1792), BF16),
            V((2, 512, 1792), BF16),
            V((2, 1792, 512), BF16),
            V((4, 16, 512), BF16),
            V((2, 16, 512), BF16),
            V((2, 256, 128), F32),
            V((2, 16, 16, 128), BF16),
            V((3, 16, 16, 128), BF16),
            V((3, 8, 128), BF16),
            V((4, 16, 8, 128), BF16),
            V((2, 128, 128), F32),
            V((4, 16, 512), BF16),
            V((4, 8, 16, 512), BF16),
            V((4, 8, 128), F32),
            V((4, 16, 8, 128), F32),
            V((4, 16, 16, 256), BF16),
            V((4, 16, 16, 256), BF16),
            V((4, 16, 128), BF16),
            V((4, 16, 16, 128), BF16),
            V((4, 16, 512), BF16),
            V((4, 8, 16, 512), BF16),
            S((5,)),
            S((12,)),
            S((7,)),
            S((7,)),
            S((2,)),
            S((3,)),
            S((3,)),
            S((4,)),
            S((4,)),
            S((4,)),
            S((4,)),
            S((4,)),
            S((4,)),
            S((4, 16)),
            S((4,)),
            S((4, 16)),
            S((4,)),
            S((4,)),
            S((2,)),
            S((2,)),
        ],
        compiler_params=pltpu.CompilerParams(
            collective_id=0, has_side_effects=True, vmem_limit_bytes=56 << 20
        ),
    )(
        lengths, owner_order, jnp.asarray(FREQS), hidden_in, attn_gain, ffn_gain,
        w_query, w_key, w_value, w_out, w_gate, w_up, w_down, key_cache, value_cache,
    )


def solution(mesh):
    placed = (
        P(None, "mem"),
        P(),
        P(),
        P("section", "mem"),
        P("section", "mem", "tp"),
        P("section", "mem", "tp"),
        P("section", "mem", "tp"),
        P("section", "tp", "mem"),
        P("section", "mem"),
        P("section", "mem", "tp"),
        P("section", "mem", "tp"),
        P("section", "tp", "mem"),
        P("section", "mem", None, "tp"),
        P("section", "mem", None, "tp"),
    )
    return jax.shard_map(
        per_device, mesh=mesh, in_specs=placed, out_specs=P("section", None, "mem"), check_vma=False
    )
```
